128 devices in a mesh: frame: 16 (over y, x), head: 4 (over z), dp: 2 (over core).
Axes of the slice: x: 4, y: 4, z: 4, core: 2. Of those that a mesh axis runs over, the one named last changes fastest.
Arguments:
- latent: bfloat16 [64, 8, 24, 5120], P(('dp', 'frame'), 'head'), parts along dimension 0, may hold values from -6 to 6, as said below
- pose_maps: bfloat16 [64, 16, 48, 256], P(('dp', 'frame'), 'head'), parts along dimension 0, may hold values from -6 to 6
- conv_weight: bfloat16 [3, 3, 3, 256, 320], replicated, may hold values from -0.078125 to 0.078125
- conv_bias: float32 [320], replicated, may hold values from -3 to 3
- pose_proj: bfloat16 [320, 5120], replicated, may hold values from -0.3125 to 0.3125
- w_qkv: bfloat16 [5120, 20, 3, 128], P('frame', 'head'), may hold values from -2 to 2
- w_out: bfloat16 [20, 128, 5120], P('head'), may hold values from -1 to 1
- clip_lengths: int32 [6], P('dp'), parts along dimension 0, may hold values from 1 to 28, 32 in all
- block_ids: int32 [64], P('dp'), parts along dimension 0, may hold values from 0 to 15, never falling along the last dimension, each value on 1 to 3 neighbouring positions
Outputs:
- attended: bfloat16 [64, 8, 24, 5120], P(('dp', 'frame'), 'head'), parts along dimension 0
The draws below stay inside these ranges and needn't reach their ends.
There are 2 independent parts, one for each index of `dp`. The reference program is written for one: setup_inputs(seed, part) draws one part's arguments, and reference() takes and returns one part's arrays. A program takes and returns all parts, laid end to end along the dimension named above; an argument that names none is the same for every part. Nothing has to cross between parts.
Inputs may be any that keep to these rules, and one draw needn't show every extreme that they name: `clip_lengths`: the clips together cover all 32 frames; the longest clip has exactly 28 frames. `block_ids`: never falls along the frames; every block id in the range is used, by at most 3 consecutive frames. `latent`: activations of order one.
All inputs are finite; a program needn't handle non-finite values.
Results may differ from the reference program's by a relative error of at most 0.017.
Values may be sent and summed in bfloat16 or wider, within the bound.
A program may use at most 128 MiB of HBM per device.

```python
import math
import jax
import jax.numpy as jnp
import numpy as np
from jax import lax

D = 5120
HEAD_DIM = 128
HEADS_DEV = 5
C_IN = 256
C_OUT = 320
HL = 8
WL = 24
CLIPS = 3
BLOCK_MOST = 3
FRAMES = 32
HEADS = 20
TOKENS = 6144
N_HEAD = 4


def draw_latent(key, part):
    shape_all = (FRAMES, HL, WL, D)
    normal_part = jax.random.normal(jax.random.fold_in(key, 11), shape_all, jnp.float32)
    return jnp.clip(normal_part, -6.0, 6.0).astype(jnp.bfloat16)


def draw_w_qkv(key, part):
    base_draw = jnp.clip(jax.random.normal(jax.random.fold_in(key, 21), (D, HEADS, 3, HEAD_DIM), jnp.float32), -4.0, 4.0) * D ** (-0.5)
    return base_draw.astype(jnp.bfloat16)


def steps_of(key, extent, split, smallest, high):
    def one(dim, shards_of):
        steps = jax.random.uniform(jax.random.fold_in(jax.random.fold_in(key, 6), dim), (shards_of,), jnp.float32, smallest / len(split), high / len(split))
        return jnp.repeat(jnp.exp(steps), extent[dim] // shards_of).reshape((-1,) + (1,) * (len(extent) - dim - 1))

    gain = one(*split[0])
    for cut in split[1:]:
        gain = gain * one(*cut)
    return gain


def length_profile(amount, total, limit, skew):
    portions = [(1 << 20) // math.isqrt(rank ** skew) + 1 for rank in range(2, amount + 1)]
    rest, counts = total - limit - (amount - 1), [1] * (amount - 1)
    while rest > 0:
        movable = [i for i in range(amount - 1) if counts[i] < limit]
        pool, budget = sum([portions[i] for i in movable]), rest
        for i in movable:
            more = min(limit - counts[i], max(1, budget * portions[i] // pool), rest)
            counts[i] = counts[i] + more
            rest = rest - more
    return np.array([limit] + counts)


def uneven_parts(key, number_of, total, reach, slope):
    if number_of == 2:
        one = jax.random.randint(key, (), max(1, total - reach), min(reach, total - 1) + 1)
        return jnp.stack([one, total - one])
    tallies = jnp.asarray(length_profile(number_of, total, reach, slope), jnp.int32)
    twos = (number_of - 1) // 2
    giver, receiver = tallies[1:1 + 2 * twos:2], tallies[2:2 + 2 * twos:2]
    margin = jnp.minimum(giver - 1, reach - receiver)
    passed = jax.random.randint(jax.random.fold_in(key, 1), (twos,), 0, 1 << 20) % (margin + 1)
    tallies = tallies.at[1:1 + 2 * twos:2].set(giver - passed).at[2:2 + 2 * twos:2].set(receiver + passed)
    return tallies[jax.random.permutation(jax.random.fold_in(key, 2), number_of)]


def noise(stream_key, dims, deviation, limit, split=(), held_as=jnp.bfloat16):
    entries = deviation * jax.random.normal(stream_key, dims, jnp.float32)
    if split:
        entries = entries * steps_of(stream_key, dims, split, -0.22, 0.18)
    return jnp.clip(entries, -limit, limit).astype(held_as)


def setup_inputs(seed: int = 0, part: int = 0) -> dict:
    keys = jax.random.split(jax.random.key(seed), 10)
    own_keys = jax.random.split(jax.random.fold_in(keys[9], part), 10)
    latent = draw_latent(jax.random.fold_in(jax.random.fold_in(keys[9], part), 71), part)
    pose_maps = noise(own_keys[1], (FRAMES, 2 * HL, 2 * WL, C_IN), 1.0, 6.0, ((0, 16), (1, 4)))
    conv_weight = noise(keys[2], (3, 3, 3, C_IN, C_OUT), (27 * C_IN) ** -0.5, 0.078125)
    conv_bias = noise(keys[3], (C_OUT,), 0.5, 3.0, (), jnp.float32)
    pose_proj = noise(keys[4], (C_OUT, D), C_OUT ** -0.5, 0.3125)
    w_qkv = draw_w_qkv(jax.random.fold_in(keys[9], 71), part)
    w_out = noise(keys[6], (HEADS, HEAD_DIM, D), (HEAD_DIM // 4) ** -0.5, 1.0, ((0, 4),))
    clip_lengths = uneven_parts(own_keys[7], CLIPS, FRAMES, FRAMES - 4, 2).astype(jnp.int32)
    block_ids = jnp.searchsorted(jnp.cumsum(uneven_parts(own_keys[8], FRAMES // 2, FRAMES, BLOCK_MOST, 0)), jnp.arange(FRAMES), side="right").astype(jnp.int32)
    return dict(latent=latent, pose_maps=pose_maps, conv_weight=conv_weight, conv_bias=conv_bias, pose_proj=pose_proj, w_qkv=w_qkv, w_out=w_out, clip_lengths=clip_lengths, block_ids=block_ids)


NEG_FILL = -1.0e30


def frame_tables(clip_lengths, frame_count):
    clip_ends = jnp.cumsum(clip_lengths).astype(jnp.int32)
    clip_starts = (clip_ends - clip_lengths).astype(jnp.int32)
    frame_index = jnp.arange(frame_count, dtype=jnp.int32)
    clip_of = jnp.sum((frame_index[:, None] >= clip_ends[None, :]).astype(jnp.int32), axis=1).astype(jnp.int32)
    clip_match = clip_of[:, None] == jnp.arange(clip_lengths.shape[0], dtype=jnp.int32)[None, :]
    start_of = jnp.sum(jnp.where(clip_match, clip_starts[None, :], 0), axis=1).astype(jnp.int32)
    return clip_of, start_of


def reference(latent, pose_maps, conv_weight, conv_bias, pose_proj, w_qkv, w_out, clip_lengths, block_ids):
    clip_of, start_of = frame_tables(clip_lengths, FRAMES)
    padded = jnp.pad(pose_maps, ((2, 0), (1, 0), (1, 0), (0, 0)))
    frame_ids = jnp.arange(FRAMES, dtype=jnp.int32)
    tap_list = []
    for step_a in range(3):
        keep_mask = (frame_ids - 2 + step_a >= start_of).astype(pose_maps.dtype)[:, None, None, None]
        frames_tap = padded[step_a:step_a + FRAMES] * keep_mask
        for step_b in range(3):
            for step_e in range(3):
                tap_list.append(frames_tap[:, step_b:step_b + 2 * HL - 1:2, step_e:step_e + 2 * WL - 1:2])
    stacked = jnp.concatenate(tap_list, axis=3)
    summed = jnp.dot(stacked, conv_weight.reshape(27 * C_IN, C_OUT), preferred_element_type=jnp.float32) + conv_bias
    feature = jax.nn.silu(summed).astype(jnp.bfloat16)
    guided = (latent.astype(jnp.float32) + jnp.dot(feature, pose_proj, preferred_element_type=jnp.float32)).astype(jnp.bfloat16)

    tokens = guided.reshape(TOKENS, D)
    projected = jnp.dot(tokens, w_qkv.reshape(D, HEADS * 3 * HEAD_DIM), preferred_element_type=jnp.float32)
    projected = projected.astype(jnp.bfloat16).reshape(TOKENS, HEADS, 3, HEAD_DIM)

    row_frame = jnp.arange(TOKENS, dtype=jnp.int32) // (HL * WL)
    frame_visible = (clip_of[:, None] == clip_of[None, :]) & (block_ids[None, :] <= block_ids[:, None])
    visible = jnp.take(jnp.take(frame_visible, row_frame, axis=0), row_frame, axis=1)

    def one_head(head_parts):
        query_rows, key_rows, value_rows = head_parts
        scores = jnp.dot(query_rows, key_rows.T, preferred_element_type=jnp.float32) * HEAD_DIM ** -0.5
        scores = jnp.where(visible, scores, NEG_FILL)
        row_top = jnp.max(scores, axis=1, keepdims=True)
        weights = jnp.where(visible, jnp.exp(scores - row_top), 0.0)
        row_total = jnp.sum(weights, axis=1, keepdims=True)
        mixed_rows = jnp.dot(weights.astype(jnp.bfloat16), value_rows, preferred_element_type=jnp.float32)
        return (mixed_rows / row_total).astype(jnp.bfloat16)

    heads_major = jnp.transpose(projected, (1, 2, 0, 3))
    attended = lax.map(one_head, (heads_major[:, 0], heads_major[:, 1], heads_major[:, 2]))

    grouped_rows = attended.reshape(N_HEAD, HEADS_DEV, TOKENS, HEAD_DIM)
    grouped_rows = jnp.transpose(grouped_rows, (0, 2, 1, 3)).reshape(N_HEAD, TOKENS, HEADS_DEV * HEAD_DIM)
    grouped_weight = w_out.reshape(N_HEAD, HEADS_DEV * HEAD_DIM, D)

    def add_group(running, group_item):
        rows_group, weight_group = group_item
        partial_low = jnp.dot(rows_group, weight_group, preferred_element_type=jnp.float32).astype(jnp.bfloat16)
        partial_low = lax.optimization_barrier(partial_low)
        return running + partial_low.astype(jnp.float32), None

    summed_out, unused = lax.scan(add_group, jnp.zeros((TOKENS, D), jnp.float32), (grouped_rows, grouped_weight))
    return summed_out.astype(jnp.bfloat16).reshape(FRAMES, HL, WL, D)
```

```python
import jax
import jax.numpy as jnp
from jax import lax
from jax.sharding import PartitionSpec as P

NEG_FILL = -1e30


def shifted(value, axis, steps):
    count = lax.axis_size(axis)
    leading, last = (max(0, -steps), min(count, count - steps))
    return lax.ppermute(value, axis, [(source, source + steps) for source in range(leading, last)])


def frame_tables(clip_lengths, frame_count):
    clip_index = jnp.arange(clip_lengths.shape[0], dtype=jnp.int32)
    earlier_clips = clip_index[None, :] <= clip_index[:, None]
    clip_ends = jnp.sum(jnp.where(earlier_clips, clip_lengths[None, :], 0), axis=1)
    clip_starts = clip_ends - clip_lengths
    frame_index = jnp.arange(frame_count, dtype=jnp.int32)
    clip_of = jnp.sum((frame_index[:, None] >= clip_ends[None, :]).astype(jnp.int32), axis=1)
    clip_match = clip_of[:, None] == jnp.arange(clip_lengths.shape[0], dtype=jnp.int32)[None, :]
    start_of = jnp.sum(jnp.where(clip_match, clip_starts[None, :], 0), axis=1)
    return (clip_of, start_of)


def guide_features(latent, pose_maps, conv_weight, conv_bias, pose_proj, start_of, first_frame):
    frames_dev = pose_maps.shape[0]
    upper_row = shifted(pose_maps[:, -1:], "head", 1)
    rows_ext = jnp.concatenate([upper_row, pose_maps], axis=1)
    left_column = jnp.zeros(rows_ext.shape[:2] + (1, rows_ext.shape[3]), rows_ext.dtype)
    cols_ext = jnp.concatenate([left_column, rows_ext], axis=2)
    earlier = shifted(cols_ext, "frame", 1)
    extended = jnp.concatenate([earlier, cols_ext], axis=0)
    out_rows = pose_maps.shape[1] // 2
    out_cols = pose_maps.shape[2] // 2
    frame_ids = first_frame + jnp.arange(frames_dev, dtype=jnp.int32)
    starts_here = lax.dynamic_slice_in_dim(start_of, first_frame, frames_dev)
    tap_list = []
    for step_a in range(3):
        keep_mask = (frame_ids - 2 + step_a >= starts_here).astype(pose_maps.dtype)[
            :, None, None, None
        ]
        frames_tap = extended[step_a : step_a + frames_dev] * keep_mask
        for step_b in range(3):
            for step_e in range(3):
                tap_list.append(
                    frames_tap[
                        :,
                        step_b : step_b + 2 * out_rows - 1 : 2,
                        step_e : step_e + 2 * out_cols - 1 : 2,
                    ]
                )
    stacked = jnp.concatenate(tap_list, axis=3)
    kernel = conv_weight.reshape(-1, conv_weight.shape[-1])
    summed = jnp.dot(stacked, kernel, preferred_element_type=jnp.float32) + conv_bias
    feature = jax.nn.silu(summed).astype(jnp.bfloat16)
    guided = latent.astype(jnp.float32) + jnp.dot(
        feature, pose_proj, preferred_element_type=jnp.float32
    )
    return guided.astype(jnp.bfloat16)


def attend_rows(queries, query_clip, query_block, keyvals, clip_of, block_ids):
    heads_dev = queries.shape[1]
    rows_query = queries.shape[0]
    head_size = queries.shape[2]
    score_scale = head_size ** (-0.5)
    start_carry = (
        jnp.full((heads_dev, rows_query), NEG_FILL, jnp.float32),
        jnp.zeros((heads_dev, rows_query), jnp.float32),
        jnp.zeros((heads_dev, rows_query, head_size), jnp.float32),
    )

    def one_frame(running, frame_item):
        frame_kv, frame_id = frame_item
        key_clip = clip_of[frame_id]
        key_block = block_ids[frame_id]
        visible = (query_clip == key_clip) & (key_block <= query_block)
        run_max, run_total, run_acc = running
        scores = (
            jnp.einsum(
                "qhd,khd->hqk", queries, frame_kv[:, :, 0], preferred_element_type=jnp.float32
            )
            * score_scale
        )
        scores = jnp.where(visible[None, :, None], scores, NEG_FILL)
        new_max = jnp.maximum(run_max, jnp.max(scores, axis=2))
        factor = jnp.exp(run_max - new_max)
        weights = jnp.where(visible[None, :, None], jnp.exp(scores - new_max[:, :, None]), 0.0)
        new_total = run_total * factor + jnp.sum(weights, axis=2)
        new_acc = run_acc * factor[:, :, None] + jnp.einsum(
            "hqk,khd->hqd",
            weights.astype(jnp.bfloat16),
            frame_kv[:, :, 1],
            preferred_element_type=jnp.float32,
        )
        running = (new_max, new_total, new_acc)
        return (running, None)

    running = start_carry
    shard_piece = lax.all_gather(keyvals, "frame", axis=0, tiled=True)
    piece_frames = shard_piece.shape[0]
    frame_list = jnp.arange(piece_frames, dtype=jnp.int32)
    running, unused = lax.scan(one_frame, running, (shard_piece, frame_list))
    run_max, run_total, run_acc = running
    normalized = run_acc / run_total[:, :, None]
    return jnp.transpose(normalized, (1, 0, 2)).astype(jnp.bfloat16)


def shards(
    latent, pose_maps, conv_weight, conv_bias, pose_proj, w_qkv, w_out, clip_lengths, block_ids
):
    frame_count = block_ids.shape[0]
    clip_of, start_of = frame_tables(clip_lengths, frame_count)
    frames_dev = latent.shape[0]
    first_frame = lax.axis_index("frame") * frames_dev
    guided = guide_features(
        latent, pose_maps, conv_weight, conv_bias, pose_proj, start_of, first_frame
    )
    whole_rows = lax.all_gather(guided, "head", axis=1, tiled=True)
    height = whole_rows.shape[1]
    width_grid = whole_rows.shape[2]
    model_width = whole_rows.shape[3]
    flat_tokens = whole_rows.reshape(-1, model_width)
    qkv_local = w_qkv.reshape(w_qkv.shape[0], -1)
    projected = jnp.dot(
        flat_tokens,
        lax.all_gather(qkv_local, "frame", axis=0, tiled=True),
        preferred_element_type=jnp.float32,
    ).astype(jnp.bfloat16)
    per_frame = height * width_grid
    heads_dev = w_qkv.shape[1]
    head_size = w_qkv.shape[3]
    grouped = projected.reshape(frames_dev, per_frame, heads_dev, 3, head_size)
    rows_total = frames_dev * per_frame
    queries = grouped[:, :, :, 0].reshape(rows_total, heads_dev, head_size)
    keyvals = grouped[:, :, :, 1:3]
    clip_rows = lax.dynamic_slice_in_dim(clip_of, first_frame, frames_dev)
    block_rows = lax.dynamic_slice_in_dim(block_ids, first_frame, frames_dev)
    query_clip = jnp.repeat(clip_rows, per_frame)
    query_block = jnp.repeat(block_rows, per_frame)
    attended = attend_rows(queries, query_clip, query_block, keyvals, clip_of, block_ids)
    by_row = attended.reshape(frames_dev, height, width_grid, heads_dev * head_size)
    by_row = jnp.transpose(by_row, (1, 0, 2, 3)).reshape(
        height, frames_dev * width_grid, heads_dev * head_size
    )
    out_weight = w_out.reshape(heads_dev * head_size, w_out.shape[2])
    rows_here = height // lax.axis_size("head")
    summed_rows = lax.psum_scatter(
        jnp.dot(by_row, out_weight, preferred_element_type=jnp.float32).astype(jnp.bfloat16),
        "head",
        scatter_dimension=0,
        tiled=True,
    ).astype(jnp.float32)
    summed_rows = summed_rows.reshape(rows_here, frames_dev, width_grid, out_weight.shape[1])
    return jnp.transpose(summed_rows, (1, 0, 2, 3)).astype(jnp.bfloat16)


def solution(mesh):
    return jax.shard_map(
        shards,
        mesh=mesh,
        in_specs=(
            P(("dp", "frame"), "head", None, None),
            P(("dp", "frame"), "head", None, None),
            P(),
            P(),
            P(),
            P("frame", "head", None, None),
            P("head", None, None),
            P("dp"),
            P("dp"),
        ),
        out_specs=P(("dp", "frame"), "head", None, None),
        check_vma=False,
    )
```

```python
import functools

import jax
import jax.numpy as jnp
from jax import lax
from jax.experimental import pallas as pl
from jax.experimental.pallas import tpu as pltpu
from jax.sharding import PartitionSpec as P

NEG_FILL = -1e30
F32 = jnp.float32
BF16 = jnp.bfloat16
THIRDS = 3
KEY_SOURCES = 2


def shifted(value, axis, steps):
    count = lax.axis_size(axis)
    leading, last = (max(0, -steps), min(count, count - steps))
    return lax.ppermute(value, axis, [(source, source + steps) for source in range(leading, last)])


def frame_tables(clip_lengths, block_ids):
    frame_count = block_ids.shape[0]
    clip_index = jnp.arange(clip_lengths.shape[0], dtype=jnp.int32)
    earlier_clips = clip_index[None, :] <= clip_index[:, None]
    clip_ends = jnp.sum(jnp.where(earlier_clips, clip_lengths[None, :], 0), axis=1)
    clip_starts = clip_ends - clip_lengths
    frame_index = jnp.arange(frame_count, dtype=jnp.int32)
    clip_of = jnp.sum((frame_index[:, None] >= clip_ends[None, :]).astype(jnp.int32), axis=1)
    clip_match = clip_of[:, None] == clip_index[None, :]
    start_of = jnp.sum(jnp.where(clip_match, clip_starts[None, :], 0), axis=1)
    seen = (clip_of[:, None] == clip_of[None, :]) & (block_ids[None, :] <= block_ids[:, None])
    stop_of = start_of + jnp.sum(seen.astype(jnp.int32), axis=1)
    return start_of, stop_of


def conv_kernel(tap_ref, kernel_ref, bias_ref, keep_ref, out_ref):
    frames_dev, out_rows, wide = 2, 2, 32
    total = jnp.zeros((frames_dev * out_rows * wide, out_ref.shape[1]), F32) + bias_ref[...]
    for a in range(3):
        part = jnp.zeros_like(total)
        for b in range(3):
            rows = jnp.concatenate(
                [tap_ref[a + d, 2 * r + b] for d in range(frames_dev) for r in range(out_rows)], axis=0
            )
            for e in range(3):
                part += lax.dot_general(
                    rows[:, e * 256 : (e + 1) * 256],
                    kernel_ref[(a * 3 + b) * 3 + e],
                    (((1,), (1,)), ((), ())),
                    preferred_element_type=F32,
                )
        total += part * keep_ref[a]
    feature = total / (1.0 + jnp.exp(-total))
    feature = feature.reshape(frames_dev * out_rows, wide, -1)[:, :24].reshape(out_ref.shape)
    out_ref[...] = feature.astype(BF16)


def pose_features(pose_maps, conv_weight, conv_bias, start_of, first_frame):
    frames_dev, rows_in, cols_in, c_in = pose_maps.shape
    cols = cols_in // 2
    pairs = pose_maps.reshape(frames_dev, rows_in, cols, 2 * c_in)
    left = jnp.pad(pairs[:, :, :-1, c_in:], ((0, 0), (0, 0), (1, 0), (0, 0)))
    own = jnp.concatenate([left, pairs], axis=3)
    own = jnp.pad(own, ((0, 0), (0, 0), (0, 32 - cols), (0, 0)))
    upper = shifted(own[:, -1:], "head", 1)
    rows_ext = jnp.concatenate([upper, own], axis=1)
    earlier = shifted(rows_ext, "frame", 1)
    taps = jnp.concatenate([earlier, rows_ext], axis=0)
    c_out = conv_weight.shape[-1]
    kernel = jnp.transpose(conv_weight, (0, 1, 2, 4, 3)).reshape(27, c_out, c_in)
    starts_here = lax.dynamic_slice_in_dim(start_of, first_frame, frames_dev)
    frame_ids = first_frame + jnp.arange(frames_dev, dtype=jnp.int32)
    keep = (frame_ids[None, :] - 2 + jnp.arange(3)[:, None] >= starts_here[None, :]).astype(F32)
    out_rows = rows_in // 2
    keep = jnp.repeat(keep, out_rows * 32, axis=1)[:, :, None]
    return pl.pallas_call(
        conv_kernel,
        out_shape=jax.ShapeDtypeStruct((frames_dev * out_rows * cols, c_out), BF16),
        compiler_params=pltpu.CompilerParams(vmem_limit_bytes=32 << 20),
        name="pose_conv",
    )(taps, kernel, conv_bias[None, :], keep)


def attend_kernel(bounds_ref, recv_ref, lo_ref, hi_ref, out_ref, top_ref, total_ref, acc_ref):
    tile = pl.program_id(0)
    per_source = 384
    rows = 2 * 128
    keys = KEY_SOURCES * per_source
    queries = recv_ref[pl.ds(2 * tile, 2), 2 * per_source :, :].reshape(rows, 128)
    top_ref[...] = jnp.full_like(top_ref, NEG_FILL)
    total_ref[...] = jnp.zeros_like(total_ref)
    acc_ref[...] = jnp.zeros_like(acc_ref)
    lo = lo_ref[...]
    hi = hi_ref[...]

    def step(index, unused):
        k = recv_ref[pl.ds(KEY_SOURCES * index, KEY_SOURCES), :per_source, :].reshape(keys, 128)
        v = recv_ref[pl.ds(KEY_SOURCES * index, KEY_SOURCES), per_source : 2 * per_source, :].reshape(keys, 128)
        scores = lax.dot_general(
            queries, k, (((1,), (1,)), ((), ())), preferred_element_type=F32
        ) * (128 ** -0.5)
        token = index * keys + lax.broadcasted_iota(jnp.int32, (rows, keys), 1)
        visible = (token >= lo) & (token < hi)
        scores = jnp.where(visible, scores, NEG_FILL)
        old = top_ref[...]
        new = jnp.maximum(old, jnp.max(scores, axis=1, keepdims=True))
        factor = jnp.exp(old - new)
        weights = jnp.where(visible, jnp.exp(scores - new), 0.0)
        top_ref[...] = new
        total_ref[...] = total_ref[...] * factor + jnp.sum(weights, axis=1, keepdims=True)
        acc_ref[...] = acc_ref[...] * factor + jnp.dot(
            weights.astype(BF16), v, preferred_element_type=F32
        )
        return unused

    lax.fori_loop(bounds_ref[0, tile], bounds_ref[1, tile], step, 0)
    out_ref[...] = (acc_ref[...] / total_ref[...]).astype(BF16)


def attend(received, start_of, stop_of):
    sources = received.shape[0]
    tiles = sources // 2
    per_frame = 192
    chunk_frames = 2 * KEY_SOURCES
    low = start_of.reshape(tiles, 4)[:, 0] // chunk_frames
    high = (stop_of.reshape(tiles, 4)[:, 3] + chunk_frames - 1) // chunk_frames
    bounds = jnp.stack([low, high])
    lo = jnp.repeat(start_of * per_frame, 64)[:, None]
    hi = jnp.repeat(stop_of * per_frame, 64)[:, None]
    rows = 256
    return pl.pallas_call(
        attend_kernel,
        out_shape=jax.ShapeDtypeStruct((tiles * rows, 128), BF16),
        grid_spec=pltpu.PrefetchScalarGridSpec(
            num_scalar_prefetch=1,
            grid=(tiles,),
            in_specs=[
                pl.BlockSpec(received.shape, lambda i, b: (0, 0, 0), pipeline_mode=pl.Buffered(1)),
                pl.BlockSpec((rows, 1), lambda i, b: (i, 0)),
                pl.BlockSpec((rows, 1), lambda i, b: (i, 0)),
            ],
            out_specs=pl.BlockSpec((rows, 128), lambda i, b: (i, 0)),
            scratch_shapes=[
                pltpu.VMEM((rows, 1), F32),
                pltpu.VMEM((rows, 1), F32),
                pltpu.VMEM((rows, 128), F32),
            ],
        ),
        compiler_params=pltpu.CompilerParams(vmem_limit_bytes=48 << 20),
        name="attend",
    )(bounds, received, lo, hi)


def shards(
    latent, pose_maps, conv_weight, conv_bias, pose_proj, w_qkv, w_out, clip_lengths, block_ids
):
    start_of, stop_of = frame_tables(clip_lengths, block_ids)
    frames_dev, rows_dev, width, model = latent.shape
    n_frame = lax.axis_size("frame")
    heads_dev, head_size = w_qkv.shape[1], w_qkv.shape[3]
    first_frame = lax.axis_index("frame") * frames_dev
    half = w_qkv.shape[0] // 2
    weight_half = lax.dynamic_slice_in_dim(
        w_qkv.reshape(w_qkv.shape[0], -1), lax.axis_index("dp") * half, half, 0
    )
    weights = lax.all_gather(weight_half, ("frame", "dp"), axis=0, tiled=True)
    latents = lax.all_gather(latent, "head", axis=1, tiled=True)
    feature = pose_features(pose_maps, conv_weight, conv_bias, start_of, first_frame)
    feature = feature.reshape(frames_dev, rows_dev, width, -1)
    features = lax.all_gather(feature, "head", axis=1, tiled=True)
    rows_total = frames_dev * latents.shape[1] * width
    guided = latents.reshape(rows_total, model).astype(F32) + jnp.dot(
        features.reshape(rows_total, -1), pose_proj, preferred_element_type=F32
    )
    guided = guided.astype(BF16)
    projected = jnp.dot(guided, weights, preferred_element_type=F32).astype(BF16)
    by_head = jnp.transpose(projected.reshape(rows_total, heads_dev, 3, head_size), (1, 2, 0, 3))
    keyvals = by_head[:, 1:].reshape(heads_dev, 1, 2 * rows_total, head_size)
    keyvals = jnp.broadcast_to(keyvals, (heads_dev, THIRDS, 2 * rows_total, head_size))
    third = latents.shape[1] * width // THIRDS
    queries = by_head[:, 0].reshape(heads_dev, frames_dev, THIRDS, third, head_size)
    queries = jnp.transpose(queries, (0, 2, 1, 3, 4)).reshape(heads_dev, THIRDS, -1, head_size)
    units = jnp.concatenate([keyvals, queries], axis=2).reshape(heads_dev * THIRDS, -1, head_size)
    units = jnp.pad(units, ((0, n_frame - heads_dev * THIRDS), (0, 0), (0, 0)))
    received = lax.all_to_all(units, "frame", 0, 0, tiled=True)
    mixed = attend(received, start_of, stop_of)
    mixed = lax.all_to_all(mixed.reshape(n_frame, -1, head_size), "frame", 0, 0, tiled=True)
    mixed = mixed[: heads_dev * THIRDS].reshape(heads_dev, THIRDS, frames_dev, third, head_size)
    mixed = jnp.transpose(mixed, (2, 1, 3, 0, 4)).reshape(frames_dev, -1, width, heads_dev * head_size)
    height = mixed.shape[1]
    by_row = jnp.transpose(mixed, (1, 0, 2, 3)).reshape(height, frames_dev * width, -1)
    out_weight = w_out.reshape(heads_dev * head_size, w_out.shape[2])
    summed_rows = lax.psum_scatter(
        jnp.dot(by_row, out_weight, preferred_element_type=F32).astype(BF16),
        "head",
        scatter_dimension=0,
        tiled=True,
    )
    summed_rows = summed_rows.reshape(rows_dev, frames_dev, width, out_weight.shape[1])
    return jnp.transpose(summed_rows, (1, 0, 2, 3))


def solution(mesh):
    return jax.shard_map(
        shards,
        mesh=mesh,
        in_specs=(
            P(("dp", "frame"), "head", None, None),
            P(("dp", "frame"), "head", None, None),
            P(),
            P(),
            P(),
            P("frame", "head", None, None),
            P("head", None, None),
            P("dp"),
            P("dp"),
        ),
        out_specs=P(("dp", "frame"), "head", None, None),
        check_vma=False,
    )
```

```python
import functools

import jax
import jax.numpy as jnp
from jax import lax
from jax.experimental import pallas as pl
from jax.experimental.pallas import tpu as pltpu
from jax.sharding import PartitionSpec as P

NEG_FILL = -1e30
F32 = jnp.float32
BF16 = jnp.bfloat16
THIRDS = 3
KEY_SOURCES = 2
MESH = pl.DeviceIdType.MESH
RING = 4
OFFSETS = (0, RING - 1, 1, 2)
PARTS = ((0, 160), (0, 80), (80, 80))
HALO, LATENT, FEATURE, WEIGHT, SIBLING, COPIES = 0, 3, 7, 10, 58, 74


def frame_tables(clip_lengths, block_ids):
    frame_count = block_ids.shape[0]
    clip_index = jnp.arange(clip_lengths.shape[0], dtype=jnp.int32)
    earlier_clips = clip_index[None, :] <= clip_index[:, None]
    clip_ends = jnp.sum(jnp.where(earlier_clips, clip_lengths[None, :], 0), axis=1)
    clip_starts = clip_ends - clip_lengths
    frame_index = jnp.arange(frame_count, dtype=jnp.int32)
    clip_of = jnp.sum((frame_index[:, None] >= clip_ends[None, :]).astype(jnp.int32), axis=1)
    clip_match = clip_of[:, None] == clip_index[None, :]
    start_of = jnp.sum(jnp.where(clip_match, clip_starts[None, :], 0), axis=1)
    seen = (clip_of[:, None] == clip_of[None, :]) & (block_ids[None, :] <= block_ids[:, None])
    stop_of = start_of + jnp.sum(seen.astype(jnp.int32), axis=1)
    return start_of, stop_of


def gather_kernel(
    own_ref, latent_ref, weight_ref, conv_ref, proj_ref, bias_ref, keep_ref,
    kv_ref, q_ref,
    taps, latents, weights, conv_w, proj, feats, guided, acc, qkv,
    send, recv, local, push_send, push_recv,
):
    f, z, c = lax.axis_index("frame"), lax.axis_index("head"), lax.axis_index("dp")
    x, y = lax.rem(f, RING), lax.div(f, RING)
    a, b = x + c * (y - x), y + c * (x - y)
    n_frame = RING * RING
    ahead, behind = lax.rem(f + 1, n_frame), lax.rem(f + n_frame - 1, n_frame)
    below, above, across = lax.rem(z + 1, RING), lax.rem(z + RING - 1, RING), lax.rem(z + 2, RING)

    def place(core, va, vb):
        va, vb = lax.rem(va, RING), lax.rem(vb, RING)
        return (vb + core * (va - vb)) * RING + va + core * (vb - va)

    locals_ = [
        pltpu.make_async_copy(own_ref, taps.at[pl.ds(2, 2), pl.ds(1, 4)], local.at[0]),
        pltpu.make_async_copy(conv_ref, conv_w, local.at[1]),
        pltpu.make_async_copy(proj_ref, proj, local.at[2]),
        pltpu.make_async_copy(latent_ref, latents.at[:, z], local.at[3]),
        pltpu.make_async_copy(
            weight_ref, weights.at[:, pl.ds(pl.multiple_of(f * 320, 320), 320), :], local.at[4]
        ),
    ]
    for copy in locals_:
        copy.start()

    barrier = pltpu.get_barrier_semaphore()

    def greet(j, unused):
        pl.semaphore_signal(
            barrier, inc=1, device_id={"frame": lax.rem(f + j, n_frame)}, device_id_type=MESH
        )
        return unused

    lax.fori_loop(1, n_frame, greet, 0)
    for other in (below, above, across):
        pl.semaphore_signal(barrier, inc=1, device_id={"head": other}, device_id_type=MESH)
    pl.semaphore_signal(barrier, inc=1, device_id={"dp": 1 - c}, device_id_type=MESH)
    pl.semaphore_signal(barrier, inc=1, device_id={"frame": ahead, "head": below}, device_id_type=MESH)
    pl.semaphore_signal(barrier, inc=1, device_id={"frame": behind, "head": above}, device_id_type=MESH)
    pl.semaphore_wait(barrier, n_frame - 1 + 3 + 1 + 2)

    copies = {}

    def start(slot, src, dst, device):
        copy = pltpu.make_async_remote_copy(
            src_ref=src, dst_ref=dst, send_sem=send.at[slot], recv_sem=recv.at[slot],
            device_id=device, device_id_type=MESH,
        )
        copy.start()
        copies[slot] = copy

    def arrived(slot):
        copies[slot].wait_recv()

    start(HALO, own_ref, taps.at[pl.ds(0, 2), pl.ds(1, 4)], {"frame": ahead})
    start(HALO + 1, own_ref.at[:, pl.ds(3, 1)], taps.at[pl.ds(2, 2), pl.ds(0, 1)], {"head": below})
    start(
        HALO + 2, own_ref.at[:, pl.ds(3, 1)], taps.at[pl.ds(0, 2), pl.ds(0, 1)],
        {"frame": ahead, "head": below},
    )

    def region(shard, core, part):
        offset, rows = PARTS[part]
        first = pl.multiple_of(shard * 320 + core * 160 + offset, 16)
        return weights.at[:, pl.ds(first, rows), :]

    def slot_of(ia, ib, part):
        return WEIGHT + 3 * (ia * 4 + ib) + part

    first_half = weight_ref.at[:, pl.ds(pl.multiple_of(c * 160, 160), 160), :]

    def pass_on(ia, ib, axis, step, part):
        shard = place(c, a + OFFSETS[ia], b + OFFSETS[ib])
        go = 1 if step > 0 else RING - 1
        device = place(c, a + go, b) if axis == 0 else place(c, a, b + go)
        was = ia if axis == 0 else ib
        now = (1 if step > 0 else 2) if was == 0 else 3
        there = (now, ib) if axis == 0 else (ia, now)
        src = region(shard, c, part)
        if ia == 0 and ib == 0:
            src = first_half
        start(slot_of(*there, part), src, region(shard, c, part), {"frame": device})

    def to_sibling(ia, ib):
        shard = place(c, a + OFFSETS[ia], b + OFFSETS[ib])
        start(SIBLING + 4 * ia + ib, region(shard, c, 0), region(shard, c, 0), {"dp": 1 - c})

    def received(ia, ib):
        for part in (1, 2) if 3 in ((ia, ib) if ib == 0 else (ib,)) else (0,):
            arrived(slot_of(ia, ib, part))
        if ib == 0:
            pass_on(ia, 0, 1, 1, 0)
            pass_on(ia, 0, 1, -1, 0)
            if ia == 1:
                pass_on(1, 0, 0, 1, 1)
            if ia == 2:
                pass_on(2, 0, 0, -1, 2)
        if ib == 1:
            pass_on(ia, 1, 1, 1, 1)
        if ib == 2:
            pass_on(ia, 2, 1, -1, 2)
        to_sibling(ia, ib)

    pass_on(0, 0, 0, 1, 0)
    pass_on(0, 0, 0, -1, 0)
    start(LATENT, latent_ref, latents.at[:, z], {"head": below})
    start(LATENT + 1, latent_ref, latents.at[:, z], {"head": above})
    pass_on(0, 0, 1, 1, 0)
    pass_on(0, 0, 1, -1, 0)

    locals_[0].wait()
    locals_[1].wait()
    for slot in (HALO, HALO + 1, HALO + 2):
        arrived(slot)

    @pl.when(z == 0)
    def _():
        taps[:, 0] = jnp.zeros_like(taps[:, 0])

    total = jnp.zeros((128, 320), F32) + bias_ref[...]
    for ta in range(3):
        part = jnp.zeros((128, 320), F32)
        for tb in range(3):
            rows = jnp.concatenate(
                [taps[ta + d, 2 * r + tb] for d in range(2) for r in range(2)], axis=0
            )
            for te in range(3):
                part += lax.dot_general(
                    rows[:, te * 256 : (te + 1) * 256], conv_w[(ta * 3 + tb) * 3 + te],
                    (((1,), (1,)), ((), ())), preferred_element_type=F32,
                )
        total += part * keep_ref[ta]
    feature = total / (1.0 + jnp.exp(-total))
    feature = feature.reshape(4, 32, 320)[:, :24].reshape(2, 48, 320)
    feats[:, z] = feature.astype(BF16)
    for i, other in enumerate((below, above, across)):
        start(FEATURE + i, feats.at[:, z], feats.at[:, z], {"head": other})

    received(1, 0)
    received(2, 0)
    received(0, 1)
    received(0, 2)
    arrived(LATENT)
    start(LATENT + 2, latents.at[0, above], latents.at[0, above], {"head": below})
    arrived(LATENT + 1)
    start(LATENT + 3, latents.at[1, below], latents.at[1, below], {"head": above})
    received(3, 0)
    received(1, 1)
    received(1, 2)
    received(2, 1)
    received(2, 2)
    for i in range(3):
        arrived(FEATURE + i)
    arrived(LATENT + 2)
    arrived(LATENT + 3)
    locals_[2].wait()
    locals_[3].wait()
    locals_[4].wait()

    feature_rows = feats[...].reshape(384, 320)
    for j in range(8):
        cols = pl.ds(640 * j, 640)
        value = latents[:, :, :, cols].reshape(384, 640).astype(F32) + jnp.dot(
            feature_rows, proj[:, cols], preferred_element_type=F32
        )
        value = value.astype(BF16)
        guided[2 * j] = value[:, :320]
        guided[2 * j + 1] = value[:, 320:]

    def project(ia, ib, first=False):
        shard = place(c, a + OFFSETS[ia], b + OFFSETS[ib])
        rows = pl.ds(pl.multiple_of(shard * 320, 64), 320)
        lhs = guided[shard]

        def pair(j, unused):
            rhs = jnp.concatenate([weights[2 * j, rows, :], weights[2 * j + 1, rows, :]], axis=1)
            out = jnp.dot(lhs, rhs, preferred_element_type=F32)
            acc[j] = out if first else acc[j] + out
            return unused

        lax.fori_loop(0, 7, pair, 0)
        out = jnp.dot(lhs, weights[14, rows, :], preferred_element_type=F32)
        acc[7, :, :128] = out if first else acc[7, :, :128] + out

    project(0, 0, True)

    def ready(ia, ib):
        shard = place(c, a + OFFSETS[ia], b + OFFSETS[ib])
        slot = SIBLING + 4 * ib + ia
        pltpu.make_async_remote_copy(
            src_ref=region(shard, 1 - c, 0), dst_ref=region(shard, 1 - c, 0),
            send_sem=send.at[slot], recv_sem=recv.at[slot],
            device_id={"dp": 1 - c}, device_id_type=MESH,
        ).wait_recv()
        project(ia, ib)

    for ia, ib in ((1, 0), (2, 0), (0, 1), (0, 2)):
        ready(ia, ib)
    received(0, 3)
    ready(3, 0)
    ready(1, 1)
    received(3, 1)
    ready(1, 2)
    received(3, 2)
    ready(2, 1)
    received(1, 3)
    ready(2, 2)
    received(2, 3)
    ready(0, 3)
    received(3, 3)
    for ia, ib in ((3, 1), (3, 2), (1, 3), (2, 3), (3, 3)):
        ready(ia, ib)

    def settle(j, unused):
        out = acc[j].astype(BF16)
        qkv[2 * j] = out[:, :128].reshape(2, 192, 128)
        qkv[2 * j + 1] = out[:, 128:].reshape(2, 192, 128)
        return unused

    lax.fori_loop(0, 7, settle, 0)
    qkv[14] = acc[7, :, :128].astype(BF16).reshape(2, 192, 128)

    def unit(m):
        m = m - lax.div(m, n_frame - 1)
        return lax.div(m, THIRDS), pl.multiple_of(64 * lax.rem(m, THIRDS), 64)

    def pushes(j):
        m = lax.rem(f + j, n_frame)
        h, t = unit(m)
        common = dict(device_id={"frame": m}, device_id_type=MESH)
        return (
            pltpu.make_async_remote_copy(
                src_ref=qkv.at[pl.ds(3 * h + 1, 2)], dst_ref=kv_ref.at[f],
                send_sem=push_send.at[0, j], recv_sem=push_recv.at[0, j], **common,
            ),
            pltpu.make_async_remote_copy(
                src_ref=qkv.at[3 * h, :, pl.ds(t, 64), :], dst_ref=q_ref.at[f],
                send_sem=push_send.at[1, j], recv_sem=push_recv.at[1, j], **common,
            ),
        )

    def push(j, unused):
        for copy in pushes(j):
            copy.start()
        return unused

    lax.fori_loop(1, n_frame, push, 0)
    h, t = unit(f)
    mine = (
        pltpu.make_async_copy(qkv.at[pl.ds(3 * h + 1, 2)], kv_ref.at[f], local.at[5]),
        pltpu.make_async_copy(qkv.at[3 * h, :, pl.ds(t, 64), :], q_ref.at[f], local.at[6]),
    )
    for copy in mine:
        copy.start()
    for copy in copies.values():
        copy.wait_send()
    for copy in mine:
        copy.wait()

    def drain(j, unused):
        for copy in pushes(j):
            copy.wait()
        return unused

    lax.fori_loop(1, n_frame, drain, 0)


def project_rows(latent, pose_maps, conv_weight, conv_bias, pose_proj, w_qkv, start_of, first_frame):
    frames_dev, rows_in, cols_in, c_in = pose_maps.shape
    cols = cols_in // 2
    pairs = pose_maps.reshape(frames_dev, rows_in, cols, 2 * c_in)
    left = jnp.pad(pairs[:, :, :-1, c_in:], ((0, 0), (0, 0), (1, 0), (0, 0)))
    own = jnp.concatenate([left, pairs], axis=3)
    own = jnp.pad(own, ((0, 0), (0, 0), (0, 32 - cols), (0, 0)))
    c_out = conv_weight.shape[-1]
    kernel = jnp.transpose(conv_weight, (0, 1, 2, 4, 3)).reshape(27, c_out, c_in)
    weight = jnp.transpose(w_qkv, (1, 2, 0, 3)).reshape(15, 320, 128)
    starts_here = lax.dynamic_slice_in_dim(start_of, first_frame, frames_dev)
    frame_ids = first_frame + jnp.arange(frames_dev, dtype=jnp.int32)
    keep = (frame_ids[None, :] - 2 + jnp.arange(3)[:, None] >= starts_here[None, :]).astype(F32)
    keep = jnp.repeat(keep, rows_in // 2 * 32, axis=1)[:, :, None]
    hbm = pl.BlockSpec(memory_space=pl.ANY)
    vmem = pl.BlockSpec(memory_space=pltpu.VMEM)
    return pl.pallas_call(
        gather_kernel,
        out_shape=(
            jax.ShapeDtypeStruct((16, 2, 2, 192, 128), BF16),
            jax.ShapeDtypeStruct((16, 2, 64, 128), BF16),
        ),
        in_specs=[hbm] * 5 + [vmem] * 2,
        out_specs=(hbm, hbm),
        scratch_shapes=[
            pltpu.VMEM((4, 5, 32, 768), BF16),
            pltpu.VMEM((2, 4, 48, 5120), BF16),
            pltpu.VMEM((15, 5120, 128), BF16),
            pltpu.VMEM((27, c_out, c_in), BF16),
            pltpu.VMEM((320, 5120), BF16),
            pltpu.VMEM((2, 4, 48, 320), BF16),
            pltpu.VMEM((16, 384, 320), BF16),
            pltpu.VMEM((8, 384, 256), F32),
            pltpu.VMEM((15, 2, 192, 128), BF16),
            pltpu.SemaphoreType.DMA((COPIES,)),
            pltpu.SemaphoreType.DMA((COPIES,)),
            pltpu.SemaphoreType.DMA((7,)),
            pltpu.SemaphoreType.DMA((2, 16)),
            pltpu.SemaphoreType.DMA((2, 16)),
        ],
        compiler_params=pltpu.CompilerParams(
            collective_id=0, has_side_effects=True, vmem_limit_bytes=56 << 20
        ),
        name="gather_project",
    )(own, latent.reshape(2, 48, 5120), weight, kernel, pose_proj, conv_bias[None, :], keep)


def attend_kernel(bounds_ref, kv_ref, q_ref, lo_ref, hi_ref, out_ref, top_ref, total_ref, acc_ref):
    tile = pl.program_id(0)
    per_source = 384
    rows = 2 * 128
    keys = KEY_SOURCES * per_source
    queries = q_ref[...].reshape(rows, 128)
    top_ref[...] = jnp.full_like(top_ref, NEG_FILL)
    total_ref[...] = jnp.zeros_like(total_ref)
    acc_ref[...] = jnp.zeros_like(acc_ref)
    lo = lo_ref[...]
    hi = hi_ref[...]

    def step(index, unused):
        k = kv_ref[pl.ds(KEY_SOURCES * index, KEY_SOURCES), 0].reshape(keys, 128)
        v = kv_ref[pl.ds(KEY_SOURCES * index, KEY_SOURCES), 1].reshape(keys, 128)
        scores = lax.dot_general(
            queries, k, (((1,), (1,)), ((), ())), preferred_element_type=F32
        ) * (128 ** -0.5)
        token = index * keys + lax.broadcasted_iota(jnp.int32, (rows, keys), 1)
        visible = (token >= lo) & (token < hi)
        scores = jnp.where(visible, scores, NEG_FILL)
        old = top_ref[...]
        new = jnp.maximum(old, jnp.max(scores, axis=1, keepdims=True))
        factor = jnp.exp(old - new)
        weights = jnp.where(visible, jnp.exp(scores - new), 0.0)
        top_ref[...] = new
        total_ref[...] = total_ref[...] * factor + jnp.sum(weights, axis=1, keepdims=True)
        acc_ref[...] = acc_ref[...] * factor + jnp.dot(
            weights.astype(BF16), v, preferred_element_type=F32
        )
        return unused

    lax.fori_loop(bounds_ref[0, tile], bounds_ref[1, tile], step, 0)
    out_ref[...] = (acc_ref[...] / total_ref[...]).astype(BF16)


def attend(keyvals, queries, start_of, stop_of):
    sources = keyvals.shape[0]
    tiles = sources // 2
    per_frame = 192
    chunk_frames = 2 * KEY_SOURCES
    low = start_of.reshape(tiles, 4)[:, 0] // chunk_frames
    high = (stop_of.reshape(tiles, 4)[:, 3] + chunk_frames - 1) // chunk_frames
    bounds = jnp.stack([low, high])
    lo = jnp.repeat(start_of * per_frame, 64)[:, None]
    hi = jnp.repeat(stop_of * per_frame, 64)[:, None]
    rows = 256
    return pl.pallas_call(
        attend_kernel,
        out_shape=jax.ShapeDtypeStruct((tiles * rows, 128), BF16),
        grid_spec=pltpu.PrefetchScalarGridSpec(
            num_scalar_prefetch=1,
            grid=(tiles,),
            in_specs=[
                pl.BlockSpec(keyvals.shape, lambda i, b: (0, 0, 0, 0), pipeline_mode=pl.Buffered(1)),
                pl.BlockSpec((2, 128, 128), lambda i, b: (i, 0, 0)),
                pl.BlockSpec((rows, 1), lambda i, b: (i, 0)),
                pl.BlockSpec((rows, 1), lambda i, b: (i, 0)),
            ],
            out_specs=pl.BlockSpec((rows, 128), lambda i, b: (i, 0)),
            scratch_shapes=[
                pltpu.VMEM((rows, 1), F32),
                pltpu.VMEM((rows, 1), F32),
                pltpu.VMEM((rows, 128), F32),
            ],
        ),
        compiler_params=pltpu.CompilerParams(vmem_limit_bytes=48 << 20),
        name="attend",
    )(bounds, keyvals, queries, lo, hi)


def shards(
    latent, pose_maps, conv_weight, conv_bias, pose_proj, w_qkv, w_out, clip_lengths, block_ids
):
    start_of, stop_of = frame_tables(clip_lengths, block_ids)
    frames_dev, rows_dev, width, model = latent.shape
    n_frame = lax.axis_size("frame")
    heads_dev, head_size = w_qkv.shape[1], w_qkv.shape[3]
    first_frame = lax.axis_index("frame") * frames_dev
    keyvals, queries = project_rows(
        latent, pose_maps, conv_weight, conv_bias, pose_proj, w_qkv, start_of, first_frame
    )
    keyvals = keyvals.reshape(n_frame, 2, -1, head_size)
    third = queries.shape[2]
    mixed = attend(keyvals, queries.reshape(n_frame, -1, head_size), start_of, stop_of)
    mixed = lax.all_to_all(mixed.reshape(n_frame, -1, head_size), "frame", 0, 0, tiled=True)
    mixed = mixed[: heads_dev * THIRDS].reshape(heads_dev, THIRDS, frames_dev, third, head_size)
    mixed = jnp.transpose(mixed, (2, 1, 3, 0, 4)).reshape(frames_dev, -1, width, heads_dev * head_size)
    height = mixed.shape[1]
    by_row = jnp.transpose(mixed, (1, 0, 2, 3)).reshape(height, frames_dev * width, -1)
    out_weight = w_out.reshape(heads_dev * head_size, w_out.shape[2])
    summed_rows = lax.psum_scatter(
        jnp.dot(by_row, out_weight, preferred_element_type=F32).astype(BF16),
        "head",
        scatter_dimension=0,
        tiled=True,
    )
    summed_rows = summed_rows.reshape(rows_dev, frames_dev, width, out_weight.shape[1])
    return jnp.transpose(summed_rows, (1, 0, 2, 3))


def solution(mesh):
    return jax.shard_map(
        shards,
        mesh=mesh,
        in_specs=(
            P(("dp", "frame"), "head", None, None),
            P(("dp", "frame"), "head", None, None),
            P(),
            P(),
            P(),
            P("frame", "head", None, None),
            P("head", None, None),
            P("dp"),
            P("dp"),
        ),
        out_specs=P(("dp", "frame"), "head", None, None),
        check_vma=False,
    )
```

```python
import jax
import jax.numpy as jnp
from jax import lax
from jax.experimental import pallas as pl
from jax.experimental.pallas import tpu as pltpu
from jax.sharding import PartitionSpec as P

NEG_FILL = -1e30
F32 = jnp.float32
BF16 = jnp.bfloat16
THIRDS = 3
MESH = pl.DeviceIdType.MESH
RING = 4
OFFSETS = (0, RING - 1, 1, 2)
PARTS = ((0, 160), (0, 80), (80, 80))
HALO, LATENT, FEATURE, WEIGHT, SIBLING, OUT, COPIES = 0, 3, 7, 10, 58, 74, 81
MASKED = -3e30
OUT_COLS = 512


def clip_bounds(table, frame):
    first = table[0]
    second = first + table[1]
    start = jnp.where(frame >= second, second, jnp.where(frame >= first, first, 0))
    stop = jnp.where(frame >= second, second + table[2], jnp.where(frame >= first, second, first))
    return start, stop


def gather_kernel(
    table, own_ref, latent_ref, weight_ref, conv_ref, proj_ref, w_out_ref, bias_ref,
    out_ref, wo_ref,
    taps, latents, weights, conv_w, proj, feats, guided, acc, qkv,
    kv_ref, q_ref, values, mixed, gathered, wo_tiles,
    send, recv, local, push_send, push_recv, back_send, back_recv, tile_sem,
):
    f, z, c = lax.axis_index("frame"), lax.axis_index("head"), lax.axis_index("dp")
    x, y = lax.rem(f, RING), lax.div(f, RING)
    a, b = x + c * (y - x), y + c * (x - y)
    n_frame = RING * RING
    ahead, behind = lax.rem(f + 1, n_frame), lax.rem(f + n_frame - 1, n_frame)
    below, above, across = lax.rem(z + 1, RING), lax.rem(z + RING - 1, RING), lax.rem(z + 2, RING)

    def place(core, va, vb):
        va, vb = lax.rem(va, RING), lax.rem(vb, RING)
        return (vb + core * (va - vb)) * RING + va + core * (vb - va)

    locals_ = [
        pltpu.make_async_copy(own_ref, taps.at[pl.ds(2, 2), pl.ds(1, 4)], local.at[0]),
        pltpu.make_async_copy(conv_ref, conv_w, local.at[1]),
        pltpu.make_async_copy(proj_ref, proj, local.at[2]),
        pltpu.make_async_copy(latent_ref, latents.at[:, z], local.at[3]),
        pltpu.make_async_copy(
            weight_ref, weights.at[:, pl.ds(pl.multiple_of(f * 320, 320), 320), :], local.at[4]
        ),
    ]
    for copy in locals_:
        copy.start()

    barrier = pltpu.get_barrier_semaphore()

    me = RING * f + z
    n_plane = RING * n_frame

    def greet(j, unused):
        other = lax.rem(me + j, n_plane)
        pl.semaphore_signal(
            barrier, inc=1,
            device_id={"frame": lax.div(other, RING), "head": lax.rem(other, RING)},
            device_id_type=MESH,
        )
        return unused

    lax.fori_loop(1, n_plane, greet, 0)
    pl.semaphore_signal(barrier, inc=1, device_id={"dp": 1 - c}, device_id_type=MESH)
    pl.semaphore_wait(barrier, n_plane)

    copies = {}

    def start(slot, src, dst, device):
        copy = pltpu.make_async_remote_copy(
            src_ref=src, dst_ref=dst, send_sem=send.at[slot], recv_sem=recv.at[slot],
            device_id=device, device_id_type=MESH,
        )
        copy.start()
        copies[slot] = copy

    def arrived(slot):
        copies[slot].wait_recv()

    start(HALO, own_ref, taps.at[pl.ds(0, 2), pl.ds(1, 4)], {"frame": ahead})
    start(HALO + 1, own_ref.at[:, pl.ds(3, 1)], taps.at[pl.ds(2, 2), pl.ds(0, 1)], {"head": below})
    start(
        HALO + 2, own_ref.at[:, pl.ds(3, 1)], taps.at[pl.ds(0, 2), pl.ds(0, 1)],
        {"frame": ahead, "head": below},
    )

    def region(shard, core, part):
        offset, rows = PARTS[part]
        first = pl.multiple_of(shard * 320 + core * 160 + offset, 16)
        return weights.at[:, pl.ds(first, rows), :]

    def slot_of(ia, ib, part):
        return WEIGHT + 3 * (ia * 4 + ib) + part

    first_half = weight_ref.at[:, pl.ds(pl.multiple_of(c * 160, 160), 160), :]

    def pass_on(ia, ib, axis, step, part):
        shard = place(c, a + OFFSETS[ia], b + OFFSETS[ib])
        go = 1 if step > 0 else RING - 1
        device = place(c, a + go, b) if axis == 0 else place(c, a, b + go)
        was = ia if axis == 0 else ib
        now = (1 if step > 0 else 2) if was == 0 else 3
        there = (now, ib) if axis == 0 else (ia, now)
        src = region(shard, c, part)
        if ia == 0 and ib == 0:
            src = first_half
        start(slot_of(*there, part), src, region(shard, c, part), {"frame": device})

    def to_sibling(ia, ib):
        shard = place(c, a + OFFSETS[ia], b + OFFSETS[ib])
        start(SIBLING + 4 * ia + ib, region(shard, c, 0), region(shard, c, 0), {"dp": 1 - c})

    def received(ia, ib):
        for part in (1, 2) if 3 in ((ia, ib) if ib == 0 else (ib,)) else (0,):
            arrived(slot_of(ia, ib, part))
        if ib == 0:
            pass_on(ia, 0, 1, 1, 0)
            pass_on(ia, 0, 1, -1, 0)
            if ia == 1:
                pass_on(1, 0, 0, 1, 1)
            if ia == 2:
                pass_on(2, 0, 0, -1, 2)
        if ib == 1:
            pass_on(ia, 1, 1, 1, 1)
        if ib == 2:
            pass_on(ia, 2, 1, -1, 2)
        to_sibling(ia, ib)

    pass_on(0, 0, 0, 1, 0)
    pass_on(0, 0, 0, -1, 0)
    start(LATENT, latent_ref, latents.at[:, z], {"head": below})
    start(LATENT + 1, latent_ref, latents.at[:, z], {"head": above})
    pass_on(0, 0, 1, 1, 0)
    pass_on(0, 0, 1, -1, 0)

    locals_[0].wait()
    locals_[1].wait()
    for slot in (HALO, HALO + 1, HALO + 2):
        arrived(slot)

    @pl.when(z == 0)
    def _():
        taps[:, 0] = jnp.zeros_like(taps[:, 0])

    total = jnp.zeros((128, 320), F32) + bias_ref[...]
    for ta in range(3):
        part = jnp.zeros((128, 320), F32)
        for tb in range(3):
            rows = jnp.concatenate(
                [taps[ta + d, 2 * r + tb] for d in range(2) for r in range(2)], axis=0
            )
            for te in range(3):
                part += lax.dot_general(
                    rows[:, te * 256 : (te + 1) * 256], conv_w[(ta * 3 + tb) * 3 + te],
                    (((1,), (1,)), ((), ())), preferred_element_type=F32,
                )
        keep = [
            (2 * f + d - 2 + ta >= clip_bounds(table, 2 * f + d)[0]).astype(F32) for d in range(2)
        ]
        row = lax.broadcasted_iota(jnp.int32, (128, 1), 0)
        total += part * jnp.where(row < 64, keep[0], keep[1])
    feature = total / (1.0 + jnp.exp(-total))
    feature = feature.reshape(4, 32, 320)[:, :24].reshape(2, 48, 320)
    feats[:, z] = feature.astype(BF16)
    for i, other in enumerate((below, above, across)):
        start(FEATURE + i, feats.at[:, z], feats.at[:, z], {"head": other})

    received(1, 0)
    received(2, 0)
    received(0, 1)
    received(0, 2)
    received(3, 0)
    arrived(LATENT)
    start(LATENT + 2, latents.at[0, above], latents.at[0, above], {"head": below})
    arrived(LATENT + 1)
    start(LATENT + 3, latents.at[1, below], latents.at[1, below], {"head": above})
    received(1, 1)
    received(1, 2)
    received(2, 1)
    received(2, 2)
    for i in range(3):
        arrived(FEATURE + i)
    arrived(LATENT + 2)
    arrived(LATENT + 3)

    def share(group, core, part):
        first, cols = ((0, 2560), (0, 1280), (1280, 1280))[part]
        return wo_ref.at[pl.ds(5 * group, 5), :, pl.ds(pl.multiple_of(2560 * core + first, 1280), cols)]

    own_half = w_out_ref.at[:, :, pl.ds(pl.multiple_of(2560 * c, 2560), 2560)]
    start(OUT, own_half, share(z, c, 0), {"head": below})
    start(OUT + 1, own_half, share(z, c, 0), {"head": above})
    locals_[2].wait()
    locals_[3].wait()
    locals_[4].wait()

    feature_rows = feats[...].reshape(384, 320)
    for j in range(8):
        cols = pl.ds(640 * j, 640)
        value = latents[:, :, :, cols].reshape(384, 640).astype(F32) + jnp.dot(
            feature_rows, proj[:, cols], preferred_element_type=F32
        )
        value = value.astype(BF16)
        guided[2 * j] = value[:, :320]
        guided[2 * j + 1] = value[:, 320:]

    def project(ia, ib, first=False):
        shard = place(c, a + OFFSETS[ia], b + OFFSETS[ib])
        rows = pl.ds(pl.multiple_of(shard * 320, 64), 320)
        lhs = guided[shard]

        def pair(j, unused):
            rhs = jnp.concatenate([weights[2 * j, rows, :], weights[2 * j + 1, rows, :]], axis=1)
            out = jnp.dot(lhs, rhs, preferred_element_type=F32)
            acc[j] = out if first else acc[j] + out
            return unused

        lax.fori_loop(0, 7, pair, 0)
        out = jnp.dot(lhs, weights[14, rows, :], preferred_element_type=F32)
        acc[7, :, :128] = out if first else acc[7, :, :128] + out

    project(0, 0, True)

    def ready(ia, ib):
        shard = place(c, a + OFFSETS[ia], b + OFFSETS[ib])
        slot = SIBLING + 4 * ib + ia
        pltpu.make_async_remote_copy(
            src_ref=region(shard, 1 - c, 0), dst_ref=region(shard, 1 - c, 0),
            send_sem=send.at[slot], recv_sem=recv.at[slot],
            device_id={"dp": 1 - c}, device_id_type=MESH,
        ).wait_recv()
        project(ia, ib)

    for ia, ib in ((1, 0), (2, 0), (0, 1), (0, 2)):
        ready(ia, ib)
    received(0, 3)
    ready(3, 0)
    ready(1, 1)
    received(3, 1)
    ready(1, 2)
    received(3, 2)
    ready(2, 1)
    received(1, 3)
    ready(2, 2)
    received(2, 3)
    ready(0, 3)
    received(3, 3)
    for ia, ib in ((3, 1), (3, 2), (1, 3), (2, 3), (3, 3)):
        ready(ia, ib)

    def settle(j, unused):
        out = acc[j].astype(BF16)
        qkv[2 * j] = out[:, :128].reshape(2, 4, 48, 128)
        qkv[2 * j + 1] = out[:, 128:].reshape(2, 4, 48, 128)
        return unused

    lax.fori_loop(0, 7, settle, 0)
    qkv[14] = acc[7, :, :128].astype(BF16).reshape(2, 4, 48, 128)

    def unit(m):
        m = m - lax.div(m, n_frame - 1)
        return lax.div(m, THIRDS), pl.multiple_of(16 * lax.rem(m, THIRDS), 16)

    def pushes(j):
        m = lax.rem(f + j, n_frame)
        h, t = unit(m)
        common = dict(device_id={"frame": m}, device_id_type=MESH)
        return (
            pltpu.make_async_remote_copy(
                src_ref=qkv.at[pl.ds(3 * h + 1, 2)], dst_ref=kv_ref.at[f],
                send_sem=push_send.at[0, j], recv_sem=push_recv.at[0, j], **common,
            ),
            pltpu.make_async_remote_copy(
                src_ref=qkv.at[3 * h, :, :, pl.ds(t, 16), :], dst_ref=q_ref.at[f],
                send_sem=push_send.at[1, j], recv_sem=push_recv.at[1, j], **common,
            ),
        )

    def push(j, unused):
        for copy in pushes(j):
            copy.start()
        return unused

    lax.fori_loop(1, n_frame, push, 0)
    h, t = unit(f)
    mine = (
        pltpu.make_async_copy(qkv.at[pl.ds(3 * h + 1, 2)], kv_ref.at[f], local.at[5]),
        pltpu.make_async_copy(qkv.at[3 * h, :, :, pl.ds(t, 16), :], q_ref.at[f], local.at[6]),
    )
    for copy in mine:
        copy.start()
    arrived(OUT)
    start(OUT + 2, share(above, c, 1), share(above, c, 1), {"head": below})
    start(OUT + 4, share(above, c, 0), share(above, c, 0), {"dp": 1 - c})
    arrived(OUT + 1)
    start(OUT + 3, share(below, c, 2), share(below, c, 2), {"head": above})
    start(OUT + 5, share(below, c, 0), share(below, c, 0), {"dp": 1 - c})
    for copy in mine:
        copy.wait()

    def drain(j, unused):
        for copy in pushes(j):
            copy.wait()
        return unused

    lax.fori_loop(1, n_frame, drain, 0)

    def turn(i, unused):
        values[i] = kv_ref[pl.ds(2 * i, 2), 1].reshape(768, 128).T
        return unused

    lax.fori_loop(0, 8, turn, 0)
    exponent = 1.4426950408889634 * 128 ** -0.5
    lane = lax.broadcasted_iota(jnp.int32, (1, 256), 1)

    def back(other):
        df, dz = lax.div(other, RING), lax.rem(other, RING)
        return pltpu.make_async_remote_copy(
            src_ref=mixed.at[df, :, dz], dst_ref=gathered.at[5 * z + h, :, pl.ds(t, 16), :],
            send_sem=back_send.at[other], recv_sem=back_recv.at[me],
            device_id={"frame": df, "head": dz}, device_id_type=MESH,
        )

    keep_own = pltpu.make_async_copy(
        mixed.at[f, :, z], gathered.at[5 * z + h, :, pl.ds(t, 16), :], local.at[8]
    )

    def tile(i, unused):
        queries = q_ref[pl.ds(2 * i, 2)].reshape(256, 128)
        low = jnp.zeros((1, 256), jnp.int32)
        high = jnp.zeros((1, 256), jnp.int32)
        for d in range(4):
            frame = 4 * i + d
            begin, end = clip_bounds(table, frame)
            block = table[8 + frame]
            later = (table[9 + frame] == block).astype(jnp.int32)
            later += (table[10 + frame] == block).astype(jnp.int32)
            inside = (lane >= 64 * d) & (lane < 64 * d + 64)
            low = jnp.where(inside, begin * 192, low)
            high = jnp.where(inside, jnp.minimum(end, frame + 1 + later) * 192, high)

        def chunk(j, carry):
            top, total, summed = carry
            keys = kv_ref[pl.ds(2 * j, 2), 0].reshape(768, 128)
            scores = lax.dot_general(
                keys, queries, (((1,), (1,)), ((), ())), preferred_element_type=F32
            )
            token = j * 768 + lax.broadcasted_iota(jnp.int32, (768, 256), 0)
            scores = jnp.where((token >= low) & (token < high), scores, MASKED)
            new = jnp.maximum(top, jnp.max(scores, axis=0, keepdims=True))
            factor = jnp.exp2((top - new) * exponent)
            weight = jnp.exp2((scores - new) * exponent)
            total = total * factor + jnp.sum(weight, axis=0, keepdims=True)
            summed = summed * factor + jnp.dot(
                values[j], weight.astype(BF16), preferred_element_type=F32
            )
            return new, total, summed

        carry = (
            jnp.full((1, 256), NEG_FILL, F32), jnp.zeros((1, 256), F32), jnp.zeros((128, 256), F32)
        )
        last = i + 2 - lax.div(i, 7)
        _, total, summed = lax.fori_loop(0, last, chunk, carry)
        rows = (summed / total).T.astype(BF16)
        mixed[pl.ds(2 * i, 2)] = rows.reshape(2, 2, 4, 16, 128)

        def give(e, unused):
            other = 8 * i + e

            @pl.when((f < n_frame - 1) & (other != me))
            def _():
                back(other).start()

            @pl.when((f < n_frame - 1) & (other == me))
            def _():
                keep_own.start()

            return unused

        lax.fori_loop(0, 8, give, 0)
        return unused

    lax.fori_loop(0, 6, tile, 0)
    arrived(OUT + 2)
    arrived(OUT + 3)
    start(OUT + 6, share(across, c, 0), share(across, c, 0), {"dp": 1 - c})
    lax.fori_loop(6, 8, tile, 0)
    for slot, group in ((OUT + 4, above), (OUT + 5, below), (OUT + 6, across)):
        pltpu.make_async_remote_copy(
            src_ref=share(group, 1 - c, 0), dst_ref=share(group, 1 - c, 0),
            send_sem=send.at[slot], recv_sem=recv.at[slot],
            device_id={"dp": 1 - c}, device_id_type=MESH,
        ).wait_recv()

    def fetch(n):
        cols = pl.ds(OUT_COLS * n, OUT_COLS)
        return [
            pltpu.make_async_copy(
                w_out_ref.at[:, :, cols] if group is z else wo_ref.at[pl.ds(5 * group, 5), :, cols],
                wo_tiles.at[n % 2, pl.ds(5 * group, 5)],
                tile_sem.at[n % 2, i],
            )
            for i, group in enumerate((z, above, below, across))
        ]

    for copy in fetch(0) + fetch(1):
        copy.start()

    def collect(other, unused):
        @pl.when((f < n_frame - 1) & (other != me))
        def _():
            back(other).wait_send()

        @pl.when((f < n_frame - 1) & (other == me))
        def _():
            keep_own.wait()

        @pl.when((other < n_plane - RING) & (other != me))
        def _():
            df, dz = lax.div(other, RING), lax.rem(other, RING)
            place_of = gathered.at[5 * dz + lax.div(df, THIRDS), :, pl.ds(pl.multiple_of(16 * lax.rem(df, THIRDS), 16), 16), :]
            pltpu.make_async_remote_copy(
                src_ref=place_of, dst_ref=place_of,
                send_sem=back_send.at[other], recv_sem=back_recv.at[other],
                device_id={"frame": df, "head": dz}, device_id_type=MESH,
            ).wait_recv()

        return unused

    lax.fori_loop(0, n_plane, collect, 0)
    lhs = jnp.concatenate([gathered[n].reshape(96, 128) for n in range(20)], axis=1)
    for n in range(5120 // OUT_COLS):
        for copy in fetch(n):
            copy.wait()
        out = jnp.dot(lhs, wo_tiles[n % 2].reshape(2560, OUT_COLS), preferred_element_type=F32)
        out_ref[:, :, OUT_COLS * n : OUT_COLS * (n + 1)] = out.astype(BF16).reshape(2, 48, OUT_COLS)
        if n + 2 < 5120 // OUT_COLS:
            for copy in fetch(n + 2):
                copy.start()
    for copy in copies.values():
        copy.wait_send()


def shards(
    latent, pose_maps, conv_weight, conv_bias, pose_proj, w_qkv, w_out, clip_lengths, block_ids
):
    frames_dev, rows_in, cols_in, c_in = pose_maps.shape
    cols = cols_in // 2
    pairs = pose_maps.reshape(frames_dev, rows_in, cols, 2 * c_in)
    left = jnp.pad(pairs[:, :, :-1, c_in:], ((0, 0), (0, 0), (1, 0), (0, 0)))
    own = jnp.concatenate([left, pairs], axis=3)
    own = jnp.pad(own, ((0, 0), (0, 0), (0, 32 - cols), (0, 0)))
    c_out = conv_weight.shape[-1]
    kernel = jnp.transpose(conv_weight, (0, 1, 2, 4, 3)).reshape(27, c_out, c_in)
    weight = jnp.transpose(w_qkv, (1, 2, 0, 3)).reshape(15, 320, 128)
    table = jnp.concatenate(
        [clip_lengths, jnp.zeros((5,), jnp.int32), block_ids, jnp.full((8,), -1, jnp.int32)]
    )
    hbm = pl.BlockSpec(memory_space=pl.ANY)
    vmem = pl.BlockSpec(memory_space=pltpu.VMEM)
    attended, _ = pl.pallas_call(
        gather_kernel,
        out_shape=(
            jax.ShapeDtypeStruct((2, 48, 5120), BF16),
            jax.ShapeDtypeStruct((20, 128, 5120), BF16),
        ),
        in_specs=[pl.BlockSpec(memory_space=pltpu.SMEM)] + [hbm] * 6 + [vmem],
        out_specs=(vmem, hbm),
        scratch_shapes=[
            pltpu.VMEM((4, 5, 32, 768), BF16),
            pltpu.VMEM((2, 4, 48, 5120), BF16),
            pltpu.VMEM((15, 5120, 128), BF16),
            pltpu.VMEM((27, c_out, c_in), BF16),
            pltpu.VMEM((320, 5120), BF16),
            pltpu.VMEM((2, 4, 48, 320), BF16),
            pltpu.VMEM((16, 384, 320), BF16),
            pltpu.VMEM((8, 384, 256), F32),
            pltpu.VMEM((15, 2, 4, 48, 128), BF16),
            pltpu.VMEM((16, 2, 2, 4, 48, 128), BF16),
            pltpu.VMEM((16, 2, 4, 16, 128), BF16),
            pltpu.VMEM((8, 128, 768), BF16),
            pltpu.VMEM((16, 2, 4, 16, 128), BF16),
            pltpu.VMEM((20, 2, 48, 128), BF16),
            pltpu.VMEM((2, 20, 128, OUT_COLS), BF16),
            pltpu.SemaphoreType.DMA((COPIES,)),
            pltpu.SemaphoreType.DMA((COPIES,)),
            pltpu.SemaphoreType.DMA((9,)),
            pltpu.SemaphoreType.DMA((2, 16)),
            pltpu.SemaphoreType.DMA((2, 16)),
            pltpu.SemaphoreType.DMA((64,)),
            pltpu.SemaphoreType.DMA((64,)),
            pltpu.SemaphoreType.DMA((2, 4)),
        ],
        compiler_params=pltpu.CompilerParams(
            collective_id=0, has_side_effects=True, vmem_limit_bytes=60 << 20
        ),
        name="gather_project_attend",
    )(
        table, own, latent.reshape(2, 48, 5120), weight, kernel, pose_proj, w_out,
        conv_bias[None, :],
    )
    return attended.reshape(latent.shape)


def solution(mesh):
    return jax.shard_map(
        shards,
        mesh=mesh,
        in_specs=(
            P(("dp", "frame"), "head", None, None),
            P(("dp", "frame"), "head", None, None),
            P(),
            P(),
            P(),
            P("frame", "head", None, None),
            P("head", None, None),
            P("dp"),
            P("dp"),
        ),
        out_specs=P(("dp", "frame"), "head", None, None),
        check_vma=False,
    )
```

```python
import jax
import jax.numpy as jnp
from jax import lax
from jax.experimental import pallas as pl
from jax.experimental.pallas import tpu as pltpu
from jax.sharding import PartitionSpec as P

NEG_FILL = -1e30
F32 = jnp.float32
BF16 = jnp.bfloat16
THIRDS = 3
MESH = pl.DeviceIdType.MESH
RING = 4
OFFSETS = (0, RING - 1, 1, 2)
PARTS = ((0, 160), (0, 80), (80, 80))
HALO, LATENT, FEATURE, OUT, WEIGHT = 0, 3, 7, 10, 22
RING_KEYS = [(i, 0, 0) for i in (1, 2, 3)] + [
    (i, j, part) for i in range(4) for j, part in ((1, 0), (2, 0), (3, 1), (3, 2))
]
SIBLING_KEYS = [(i, j) for i in range(4) for j in range(4) if i or j]
CHUNK = len(RING_KEYS) + len(SIBLING_KEYS)
CHUNKS = 1
HEADS_DEV = 5
COPIES = WEIGHT + CHUNKS * CHUNK
MASKED = -3e30
OUT_COLS = 512


def clip_bounds(table, frame):
    first = table[0]
    second = first + table[1]
    start = jnp.where(frame >= second, second, jnp.where(frame >= first, first, 0))
    stop = jnp.where(frame >= second, second + table[2], jnp.where(frame >= first, second, first))
    return start, stop


def gather_kernel(
    table, own_ref, latent_ref, weight_ref, conv_ref, proj_ref, w_out_ref, bias_ref,
    out_ref, wo_ref,
    taps, latents, weights, conv_w, proj, feats, guided, qkv,
    kv_ref, q_ref, values, mixed, gathered, gathered_other, wo_tiles, staged,
    send, recv, local, push_send, push_recv, back_send, back_recv, tile_sem,
):
    f, z, c = lax.axis_index("frame"), lax.axis_index("head"), lax.axis_index("dp")
    x, y = lax.rem(f, RING), lax.div(f, RING)
    a, b = x + c * (y - x), y + c * (x - y)
    n_frame = RING * RING
    ahead, behind = lax.rem(f + 1, n_frame), lax.rem(f + n_frame - 1, n_frame)
    below, above, across = lax.rem(z + 1, RING), lax.rem(z + RING - 1, RING), lax.rem(z + 2, RING)

    def place(core, va, vb):
        va, vb = lax.rem(va, RING), lax.rem(vb, RING)
        return (vb + core * (va - vb)) * RING + va + core * (vb - va)

    locals_ = [
        pltpu.make_async_copy(own_ref, taps.at[pl.ds(2, 2), pl.ds(1, 4)], local.at[0]),
        pltpu.make_async_copy(conv_ref, conv_w, local.at[1]),
        pltpu.make_async_copy(proj_ref, proj, local.at[2]),
        pltpu.make_async_copy(latent_ref, latents.at[:, z], local.at[3]),
        pltpu.make_async_copy(
            weight_ref, weights.at[:, pl.ds(pl.multiple_of(f * 320, 320), 320), :], local.at[4]
        ),
    ]
    for copy in locals_:
        copy.start()

    barrier = pltpu.get_barrier_semaphore()

    me = RING * f + z
    n_plane = RING * n_frame

    def greet(j, unused):
        other = lax.rem(me + j, n_plane)
        pl.semaphore_signal(
            barrier, inc=1,
            device_id={"frame": lax.div(other, RING), "head": lax.rem(other, RING)},
            device_id_type=MESH,
        )
        return unused

    lax.fori_loop(1, n_plane, greet, 0)
    pl.semaphore_signal(barrier, inc=1, device_id={"dp": 1 - c}, device_id_type=MESH)
    pl.semaphore_wait(barrier, n_plane)

    copies = {}

    def start(slot, src, dst, device):
        copy = pltpu.make_async_remote_copy(
            src_ref=src, dst_ref=dst, send_sem=send.at[slot], recv_sem=recv.at[slot],
            device_id=device, device_id_type=MESH,
        )
        copy.start()
        copies[slot] = copy

    def arrived(slot):
        copies[slot].wait_recv()

    start(HALO, own_ref, taps.at[pl.ds(0, 2), pl.ds(1, 4)], {"frame": ahead})
    start(HALO + 1, own_ref.at[:, pl.ds(3, 1)], taps.at[pl.ds(2, 2), pl.ds(0, 1)], {"head": below})
    start(
        HALO + 2, own_ref.at[:, pl.ds(3, 1)], taps.at[pl.ds(0, 2), pl.ds(0, 1)],
        {"frame": ahead, "head": below},
    )

    def region(g, shard, core, part):
        offset, rows = PARTS[part]
        first = pl.multiple_of(shard * 320 + core * 160 + offset, 16)
        return weights.at[:, pl.ds(first, rows), :]

    def slot_of(g, ia, ib, part):
        return WEIGHT + CHUNK * g + RING_KEYS.index((ia, ib, part))

    def sibling_slot(g, ia, ib):
        return WEIGHT + CHUNK * g + len(RING_KEYS) + SIBLING_KEYS.index((ia, ib))

    def pass_on(g, ia, ib, axis, step, part):
        shard = place(c, a + OFFSETS[ia], b + OFFSETS[ib])
        go = step % RING
        device = place(c, a + go, b) if axis == 0 else place(c, a, b + go)
        was = ia if axis == 0 else ib
        now = {1: 1, -1: 2, 2: 3}[step] if was == 0 else 3
        there = (now, ib) if axis == 0 else (ia, now)
        src = region(g, shard, c, part)
        if ia == 0 and ib == 0:
            src = weight_ref.at[:, pl.ds(pl.multiple_of(c * 160, 160), 160), :]
        start(slot_of(g, *there, part), src, region(g, shard, c, part), {"frame": device})

    def to_sibling(g, ia, ib):
        shard = place(c, a + OFFSETS[ia], b + OFFSETS[ib])
        here = region(g, shard, c, 0)
        start(sibling_slot(g, ia, ib), here, here, {"dp": 1 - c})

    def second_ring(g, ia):
        for ib, step, part in ((1, 1, 1), (2, -1, 2)):
            arrived(slot_of(g, ia, ib, 0))
            pass_on(g, ia, ib, 1, step, part)
            to_sibling(g, ia, ib)

    def last_shard(g, ia):
        arrived(slot_of(g, ia, 3, 1))
        arrived(slot_of(g, ia, 3, 2))
        to_sibling(g, ia, 3)

    def stage0(g):
        for step in (1, -1, 2):
            pass_on(g, 0, 0, 0, step, 0)
        for step in (1, -1):
            pass_on(g, 0, 0, 1, step, 0)

    def stage1(g):
        for ia in (1, 2, 3):
            arrived(slot_of(g, ia, 0, 0))
            pass_on(g, ia, 0, 1, 1, 0)
            pass_on(g, ia, 0, 1, -1, 0)
            to_sibling(g, ia, 0)
        second_ring(g, 0)

    def stage2(g):
        for ia in (1, 2, 3):
            second_ring(g, ia)
        last_shard(g, 0)

    def stage3(g):
        for ia in (1, 2, 3):
            last_shard(g, ia)

    stage0(0)
    start(LATENT, latent_ref, latents.at[:, z], {"head": below})
    start(LATENT + 1, latent_ref, latents.at[:, z], {"head": above})

    locals_[0].wait()
    locals_[1].wait()
    for slot in (HALO, HALO + 1, HALO + 2):
        arrived(slot)

    @pl.when(z == 0)
    def _():
        taps[:, 0] = jnp.zeros_like(taps[:, 0])

    total = jnp.zeros((128, 320), F32) + bias_ref[...]
    for ta in range(3):
        part = jnp.zeros((128, 320), F32)
        for tb in range(3):
            rows = jnp.concatenate(
                [taps[ta + d, 2 * r + tb] for d in range(2) for r in range(2)], axis=0
            )
            for te in range(3):
                part += lax.dot_general(
                    rows[:, te * 256 : (te + 1) * 256], conv_w[(ta * 3 + tb) * 3 + te],
                    (((1,), (1,)), ((), ())), preferred_element_type=F32,
                )
        keep = [
            (2 * f + d - 2 + ta >= clip_bounds(table, 2 * f + d)[0]).astype(F32) for d in range(2)
        ]
        row = lax.broadcasted_iota(jnp.int32, (128, 1), 0)
        total += part * jnp.where(row < 64, keep[0], keep[1])
    feature = total / (1.0 + jnp.exp(-total))
    feature = feature.reshape(4, 32, 320)[:, :24].reshape(2, 48, 320)
    feats[:, z] = feature.astype(BF16)
    for i, other in enumerate((below, above, across)):
        start(FEATURE + i, feats.at[:, z], feats.at[:, z], {"head": other})

    stage1(0)
    arrived(LATENT)
    start(LATENT + 2, latents.at[0, above], latents.at[0, above], {"head": below})
    arrived(LATENT + 1)
    start(LATENT + 3, latents.at[1, below], latents.at[1, below], {"head": above})

    def share(group, part):
        return wo_ref.at[pl.ds(5 * group, 5), :, pl.ds(1280 * part, 1280)]

    def send_share(slot, part, device):
        cols = pl.ds(pl.multiple_of(2560 * c + 1280 * part, 1280), 1280)
        start(slot, w_out_ref.at[:, :, cols], share(z, part), {"head": device})

    send_share(OUT, 0, below)
    send_share(OUT + 1, 1, above)
    stage2(0)
    for i in range(3):
        arrived(FEATURE + i)
    arrived(LATENT + 2)
    arrived(LATENT + 3)

    locals_[2].wait()
    locals_[3].wait()
    locals_[4].wait()

    feature_rows = feats[...].reshape(384, 320)
    for j in range(4):
        cols = pl.ds(1280 * j, 1280)
        value = latents[:, :, :, cols].reshape(384, 1280).astype(F32) + jnp.dot(
            feature_rows, proj[:, cols], preferred_element_type=F32
        )
        guided[j] = value.astype(BF16)

    t = pl.multiple_of(16 * lax.rem(f, THIRDS), 16)
    h = lax.div(f, THIRDS)

    def pushes(g, k):
        m = THIRDS * g + k
        common = dict(device_id={"frame": m}, device_id_type=MESH)
        return (
            pltpu.make_async_remote_copy(
                src_ref=qkv.at[pl.ds(3 * g + 1, 2)], dst_ref=kv_ref.at[f],
                send_sem=push_send.at[0, m], recv_sem=push_recv.at[0, f], **common,
            ),
            pltpu.make_async_remote_copy(
                src_ref=qkv.at[3 * g, :, :, pl.ds(16 * k, 16), :], dst_ref=q_ref.at[f],
                send_sem=push_send.at[1, m], recv_sem=push_recv.at[1, f], **common,
            ),
        )

    def stays(g, k):
        return (
            pltpu.make_async_copy(qkv.at[pl.ds(3 * g + 1, 2)], kv_ref.at[f], local.at[5]),
            pltpu.make_async_copy(qkv.at[3 * g, :, :, pl.ds(16 * k, 16), :], q_ref.at[f], local.at[6]),
        )

    stage3(0)
    for ia, ib in SIBLING_KEYS:
        slot = sibling_slot(0, ia, ib)
        there = region(0, place(1 - c, b + OFFSETS[ia], a + OFFSETS[ib]), 1 - c, 0)
        pltpu.make_async_remote_copy(
            src_ref=there, dst_ref=there, send_sem=send.at[slot], recv_sem=recv.at[slot],
            device_id={"dp": 1 - c}, device_id_type=MESH,
        ).wait_recv()

    def project(n, unused):
        g = lax.rem(f + n, HEADS_DEV)
        out = None
        for j in range(4):
            rows = pl.ds(1280 * j, 1280)
            rhs = jnp.concatenate([weights[3 * g + i, rows, :] for i in range(3)], axis=1)
            term = jnp.dot(guided[j], rhs, preferred_element_type=F32)
            out = term if out is None else out + term
        for i in range(3):
            qkv[3 * g + i] = out[:, 128 * i : 128 * (i + 1)].astype(BF16).reshape(2, 4, 48, 128)
        for k in range(THIRDS):
            m = THIRDS * g + k

            @pl.when(f != m)
            def _():
                for copy in pushes(g, k):
                    copy.start()

            @pl.when(f == m)
            def _():
                for copy in stays(g, k):
                    copy.start()

        return unused

    lax.fori_loop(0, HEADS_DEV, project, 0)
    arrived(OUT)
    start(OUT + 4, share(above, 0), share(above, 0), {"head": below})
    send_share(OUT + 2, 1, below)
    arrived(OUT + 1)
    start(OUT + 5, share(below, 1), share(below, 1), {"head": above})
    send_share(OUT + 3, 0, above)
    attends = 1 - lax.div(f, n_frame - 1)

    def land(source, unused):
        @pl.when(source != f)
        def _():
            for ref, which in ((kv_ref, 0), (q_ref, 1)):
                pltpu.make_async_remote_copy(
                    src_ref=ref.at[source], dst_ref=ref.at[source],
                    send_sem=push_send.at[which, source], recv_sem=push_recv.at[which, source],
                    device_id={"frame": source}, device_id_type=MESH,
                ).wait_recv()

        @pl.when(source == f)
        def _():
            for copy in stays(0, 0):
                copy.wait()

        return unused

    lax.fori_loop(0, n_frame * attends, land, 0)

    def turn(i, unused):
        values[i] = kv_ref[pl.ds(2 * i, 2), 1].reshape(768, 128).T
        return unused

    lax.fori_loop(0, 8 * attends, turn, 0)
    exponent = 1.4426950408889634 * 128 ** -0.5
    lane = lax.broadcasted_iota(jnp.int32, (1, 256), 1)

    def back(other):
        df, dz = lax.div(other, RING), lax.rem(other, RING)
        return pltpu.make_async_remote_copy(
            src_ref=mixed.at[df, :, dz], dst_ref=gathered.at[5 * z + h, :, pl.ds(t, 16), :],
            send_sem=back_send.at[other], recv_sem=back_recv.at[me],
            device_id={"frame": df, "head": dz}, device_id_type=MESH,
        )

    keep_own = pltpu.make_async_copy(
        mixed.at[f, :, z], gathered.at[5 * z + h, :, pl.ds(t, 16), :], local.at[8]
    )

    def tile(i, unused):
        queries = q_ref[pl.ds(2 * i, 2)].reshape(256, 128)
        low = jnp.zeros((1, 256), jnp.int32)
        high = jnp.zeros((1, 256), jnp.int32)
        for d in range(4):
            frame = 4 * i + d
            begin, end = clip_bounds(table, frame)
            block = table[8 + frame]
            later = (table[9 + frame] == block).astype(jnp.int32)
            later += (table[10 + frame] == block).astype(jnp.int32)
            inside = (lane >= 64 * d) & (lane < 64 * d + 64)
            low = jnp.where(inside, begin * 192, low)
            high = jnp.where(inside, jnp.minimum(end, frame + 1 + later) * 192, high)

        def chunk(j, carry):
            top, total, summed = carry
            keys = kv_ref[pl.ds(2 * j, 2), 0].reshape(768, 128)
            scores = lax.dot_general(
                keys, queries, (((1,), (1,)), ((), ())), preferred_element_type=F32
            )
            token = j * 768 + lax.broadcasted_iota(jnp.int32, (768, 256), 0)
            scores = jnp.where((token >= low) & (token < high), scores, MASKED)
            new = jnp.maximum(top, jnp.max(scores, axis=0, keepdims=True))
            factor = jnp.exp2((top - new) * exponent)
            weight = jnp.exp2((scores - new) * exponent)
            total = total * factor + jnp.sum(weight, axis=0, keepdims=True)
            summed = summed * factor + jnp.dot(
                values[j], weight.astype(BF16), preferred_element_type=F32
            )
            return new, total, summed

        carry = (
            jnp.full((1, 256), NEG_FILL, F32), jnp.zeros((1, 256), F32), jnp.zeros((128, 256), F32)
        )
        last = i + 2 - lax.div(i, 7)
        _, total, summed = lax.fori_loop(0, last, chunk, carry)
        rows = (summed / total).T.astype(BF16)
        mixed[pl.ds(2 * i, 2)] = rows.reshape(2, 2, 4, 16, 128)

        def give(e, unused):
            other = 8 * i + e

            @pl.when((f < n_frame - 1) & (other != me))
            def _():
                back(other).start()

            @pl.when((f < n_frame - 1) & (other == me))
            def _():
                keep_own.start()

            return unused

        lax.fori_loop(0, 8, give, 0)
        return unused

    lax.fori_loop(0, 8 * attends, tile, 0)
    for slot in range(OUT + 2, OUT + 6):
        arrived(slot)

    def half_cols(core, n):
        return pl.ds(pl.multiple_of(2560 * core + OUT_COLS * n, OUT_COLS), OUT_COLS)

    def fetch(n):
        cols = pl.ds(OUT_COLS * n, OUT_COLS)
        return [
            pltpu.make_async_copy(
                w_out_ref.at[:, :, half_cols(c, n)] if group is z
                else wo_ref.at[pl.ds(5 * group, 5), :, cols],
                wo_tiles.at[n % 2, pl.ds(5 * group, 5)],
                tile_sem.at[n % 2, i],
            )
            for i, group in enumerate((z, above, below, across))
        ]

    for copy in fetch(0) + fetch(1):
        copy.start()

    def collect(other, unused):
        @pl.when((f < n_frame - 1) & (other != me))
        def _():
            back(other).wait_send()

        @pl.when((f < n_frame - 1) & (other == me))
        def _():
            keep_own.wait()

        @pl.when((other < n_plane - RING) & (other != me))
        def _():
            df, dz = lax.div(other, RING), lax.rem(other, RING)
            place_of = gathered.at[5 * dz + lax.div(df, THIRDS), :, pl.ds(pl.multiple_of(16 * lax.rem(df, THIRDS), 16), 16), :]
            pltpu.make_async_remote_copy(
                src_ref=place_of, dst_ref=place_of,
                send_sem=back_send.at[other], recv_sem=back_recv.at[other],
                device_id={"frame": df, "head": dz}, device_id_type=MESH,
            ).wait_recv()

        return unused

    lax.fori_loop(0, n_plane, collect, 0)
    start(OUT + 6, gathered, gathered_other, {"dp": 1 - c})
    arrived(OUT + 6)
    lhs = jnp.concatenate(
        [
            jnp.concatenate([ref[n].reshape(96, 128) for n in range(20)], axis=1)
            for ref in (gathered, gathered_other)
        ],
        axis=0,
    )
    n_tiles = 2560 // OUT_COLS
    for n in range(n_tiles):
        for copy in fetch(n):
            copy.wait()
        out = jnp.dot(lhs, wo_tiles[n % 2].reshape(2560, OUT_COLS), preferred_element_type=F32)
        out = out.astype(BF16).reshape(4, 48, OUT_COLS)
        staged[n] = out[2:]
        start(OUT + 7 + n, staged.at[n], out_ref.at[:, :, half_cols(c, n)], {"dp": 1 - c})
        out_ref[:, :, half_cols(c, n)] = out[:2]
        if n + 2 < n_tiles:
            for copy in fetch(n + 2):
                copy.start()
    for n in range(n_tiles):
        arrived(OUT + 7 + n)
    for copy in copies.values():
        copy.wait_send()
    for g in range(HEADS_DEV):
        for k in range(THIRDS):

            @pl.when(f != THIRDS * g + k)
            def _():
                for copy in pushes(g, k):
                    copy.wait_send()


def shards(
    latent, pose_maps, conv_weight, conv_bias, pose_proj, w_qkv, w_out, clip_lengths, block_ids
):
    frames_dev, rows_in, cols_in, c_in = pose_maps.shape
    cols = cols_in // 2
    pairs = pose_maps.reshape(frames_dev, rows_in, cols, 2 * c_in)
    left = jnp.pad(pairs[:, :, :-1, c_in:], ((0, 0), (0, 0), (1, 0), (0, 0)))
    own = jnp.concatenate([left, pairs], axis=3)
    own = jnp.pad(own, ((0, 0), (0, 0), (0, 32 - cols), (0, 0)))
    c_out = conv_weight.shape[-1]
    kernel = jnp.transpose(conv_weight, (0, 1, 2, 4, 3)).reshape(27, c_out, c_in)
    weight = jnp.transpose(w_qkv, (1, 2, 0, 3)).reshape(15, 320, 128)
    table = jnp.concatenate(
        [clip_lengths, jnp.zeros((5,), jnp.int32), block_ids, jnp.full((8,), -1, jnp.int32)]
    )
    hbm = pl.BlockSpec(memory_space=pl.ANY)
    vmem = pl.BlockSpec(memory_space=pltpu.VMEM)
    attended, _ = pl.pallas_call(
        gather_kernel,
        out_shape=(
            jax.ShapeDtypeStruct((2, 48, 5120), BF16),
            jax.ShapeDtypeStruct((20, 128, 2560), BF16),
        ),
        in_specs=[pl.BlockSpec(memory_space=pltpu.SMEM)] + [hbm] * 6 + [vmem],
        out_specs=(vmem, hbm),
        scratch_shapes=[
            pltpu.VMEM((4, 5, 32, 768), BF16),
            pltpu.VMEM((2, 4, 48, 5120), BF16),
            pltpu.VMEM((15, 5120, 128), BF16),
            pltpu.VMEM((27, c_out, c_in), BF16),
            pltpu.VMEM((320, 5120), BF16),
            pltpu.VMEM((2, 4, 48, 320), BF16),
            pltpu.VMEM((4, 384, 1280), BF16),
            pltpu.VMEM((15, 2, 4, 48, 128), BF16),
            pltpu.VMEM((16, 2, 2, 4, 48, 128), BF16),
            pltpu.VMEM((16, 2, 4, 16, 128), BF16),
            pltpu.VMEM((8, 128, 768), BF16),
            pltpu.VMEM((16, 2, 4, 16, 128), BF16),
            pltpu.VMEM((20, 2, 48, 128), BF16),
            pltpu.VMEM((20, 2, 48, 128), BF16),
            pltpu.VMEM((2, 20, 128, OUT_COLS), BF16),
            pltpu.VMEM((2560 // OUT_COLS, 2, 48, OUT_COLS), BF16),
            pltpu.SemaphoreType.DMA((COPIES,)),
            pltpu.SemaphoreType.DMA((COPIES,)),
            pltpu.SemaphoreType.DMA((9,)),
            pltpu.SemaphoreType.DMA((2, 16)),
            pltpu.SemaphoreType.DMA((2, 16)),
            pltpu.SemaphoreType.DMA((64,)),
            pltpu.SemaphoreType.DMA((64,)),
            pltpu.SemaphoreType.DMA((2, 4)),
        ],
        compiler_params=pltpu.CompilerParams(
            collective_id=0, has_side_effects=True, vmem_limit_bytes=60 << 20
        ),
        name="gather_project_attend",
    )(
        table, own, latent.reshape(2, 48, 5120), weight, kernel, pose_proj, w_out,
        conv_bias[None, :],
    )
    return attended.reshape(latent.shape)


def solution(mesh):
    return jax.shard_map(
        shards,
        mesh=mesh,
        in_specs=(
            P(("dp", "frame"), "head", None, None),
            P(("dp", "frame"), "head", None, None),
            P(),
            P(),
            P(),
            P("frame", "head", None, None),
            P("head", None, None),
            P("dp"),
            P("dp"),
        ),
        out_specs=P(("dp", "frame"), "head", None, None),
        check_vma=False,
    )
```

```python
import jax
import jax.numpy as jnp
from jax import lax
from jax.experimental import pallas as pl
from jax.experimental.pallas import tpu as pltpu
from jax.sharding import PartitionSpec as P

NEG_FILL = -1e30
F32 = jnp.float32
BF16 = jnp.bfloat16
THIRDS = 3
MESH = pl.DeviceIdType.MESH
RING = 4
OFFSETS = (0, RING - 1, 1, 2)
PARTS = ((0, 160), (0, 80), (80, 80))
HALO, LATENT, FEATURE, OUT, WEIGHT = 0, 3, 7, 10, 22
RING_KEYS = [(i, 0, 0) for i in (1, 2, 3)] + [
    (i, j, part) for i in range(4) for j, part in ((1, 0), (2, 0), (3, 1), (3, 2))
]
SIBLING_KEYS = [(i, j) for i in range(4) for j in range(4) if i or j]
CHUNK = len(RING_KEYS) + len(SIBLING_KEYS)
CHUNKS = 1
HEADS_DEV = 5
COPIES = WEIGHT + CHUNKS * CHUNK
MASKED = -3e30
OUT_COLS = 512


def clip_bounds(table, frame):
    first = table[0]
    second = first + table[1]
    start = jnp.where(frame >= second, second, jnp.where(frame >= first, first, 0))
    stop = jnp.where(frame >= second, second + table[2], jnp.where(frame >= first, second, first))
    return start, stop


def gather_kernel(
    table, own_ref, latent_ref, weight_ref, conv_ref, proj_ref, w_out_ref, bias_ref,
    out_ref, wo_ref,
    taps, latents, weights, conv_w, proj, feats, guided, qkv,
    kv_ref, q_ref, values, mixed, gathered, gathered_other, wo_tiles, staged,
    send, recv, local, push_send, push_recv, back_send, back_recv, tile_sem,
):
    f, z, c = lax.axis_index("frame"), lax.axis_index("head"), lax.axis_index("dp")
    x, y = lax.rem(f, RING), lax.div(f, RING)
    a, b = x + c * (y - x), y + c * (x - y)
    n_frame = RING * RING
    ahead, behind = lax.rem(f + 1, n_frame), lax.rem(f + n_frame - 1, n_frame)
    below, above, across = lax.rem(z + 1, RING), lax.rem(z + RING - 1, RING), lax.rem(z + 2, RING)

    def place(core, va, vb):
        va, vb = lax.rem(va, RING), lax.rem(vb, RING)
        return (vb + core * (va - vb)) * RING + va + core * (vb - va)

    locals_ = [
        pltpu.make_async_copy(own_ref, taps.at[pl.ds(2, 2), pl.ds(1, 4)], local.at[0]),
        pltpu.make_async_copy(conv_ref, conv_w, local.at[1]),
        pltpu.make_async_copy(proj_ref, proj, local.at[2]),
        pltpu.make_async_copy(latent_ref, latents.at[:, z], local.at[3]),
        pltpu.make_async_copy(
            weight_ref, weights.at[:, pl.ds(pl.multiple_of(f * 320, 320), 320), :], local.at[4]
        ),
    ]
    for copy in locals_:
        copy.start()

    barrier = pltpu.get_barrier_semaphore()

    me = RING * f + z
    n_plane = RING * n_frame

    def greet(j, unused):
        other = lax.rem(me + j, n_plane)
        pl.semaphore_signal(
            barrier, inc=1,
            device_id={"frame": lax.div(other, RING), "head": lax.rem(other, RING)},
            device_id_type=MESH,
        )
        return unused

    lax.fori_loop(1, n_plane, greet, 0)
    pl.semaphore_signal(barrier, inc=1, device_id={"dp": 1 - c}, device_id_type=MESH)
    pl.semaphore_wait(barrier, n_plane)

    copies = {}

    def start(slot, src, dst, device):
        copy = pltpu.make_async_remote_copy(
            src_ref=src, dst_ref=dst, send_sem=send.at[slot], recv_sem=recv.at[slot],
            device_id=device, device_id_type=MESH,
        )
        copy.start()
        copies[slot] = copy

    def arrived(slot):
        copies[slot].wait_recv()

    start(HALO, own_ref, taps.at[pl.ds(0, 2), pl.ds(1, 4)], {"frame": ahead})
    start(HALO + 1, own_ref.at[:, pl.ds(3, 1)], taps.at[pl.ds(2, 2), pl.ds(0, 1)], {"head": below})
    start(
        HALO + 2, own_ref.at[:, pl.ds(3, 1)], taps.at[pl.ds(0, 2), pl.ds(0, 1)],
        {"frame": ahead, "head": below},
    )

    def region(g, shard, core, part):
        offset, rows = PARTS[part]
        first = pl.multiple_of(shard * 320 + core * 160 + offset, 16)
        return weights.at[:, pl.ds(first, rows), :]

    def slot_of(g, ia, ib, part):
        return WEIGHT + CHUNK * g + RING_KEYS.index((ia, ib, part))

    def sibling_slot(g, ia, ib):
        return WEIGHT + CHUNK * g + len(RING_KEYS) + SIBLING_KEYS.index((ia, ib))

    def pass_on(g, ia, ib, axis, step, part):
        shard = place(c, a + OFFSETS[ia], b + OFFSETS[ib])
        go = step % RING
        device = place(c, a + go, b) if axis == 0 else place(c, a, b + go)
        was = ia if axis == 0 else ib
        now = {1: 1, -1: 2, 2: 3}[step] if was == 0 else 3
        there = (now, ib) if axis == 0 else (ia, now)
        src = region(g, shard, c, part)
        if ia == 0 and ib == 0:
            src = weight_ref.at[:, pl.ds(pl.multiple_of(c * 160, 160), 160), :]
        start(slot_of(g, *there, part), src, region(g, shard, c, part), {"frame": device})

    def to_sibling(g, ia, ib):
        shard = place(c, a + OFFSETS[ia], b + OFFSETS[ib])
        here = region(g, shard, c, 0)
        start(sibling_slot(g, ia, ib), here, here, {"dp": 1 - c})

    def second_ring(g, ia):
        for ib, step, part in ((1, 1, 1), (2, -1, 2)):
            arrived(slot_of(g, ia, ib, 0))
            pass_on(g, ia, ib, 1, step, part)
            to_sibling(g, ia, ib)

    def last_shard(g, ia):
        arrived(slot_of(g, ia, 3, 1))
        arrived(slot_of(g, ia, 3, 2))
        to_sibling(g, ia, 3)

    def stage0(g):
        for step in (1, -1, 2):
            pass_on(g, 0, 0, 0, step, 0)
        for step in (1, -1):
            pass_on(g, 0, 0, 1, step, 0)

    def stage1(g):
        for ia in (1, 2, 3):
            arrived(slot_of(g, ia, 0, 0))
            pass_on(g, ia, 0, 1, 1, 0)
            pass_on(g, ia, 0, 1, -1, 0)
            to_sibling(g, ia, 0)
        second_ring(g, 0)

    def stage2(g):
        for ia in (1, 2, 3):
            second_ring(g, ia)
        last_shard(g, 0)

    def stage3(g):
        for ia in (1, 2, 3):
            last_shard(g, ia)

    stage0(0)
    start(LATENT, latent_ref, latents.at[:, z], {"head": below})
    start(LATENT + 1, latent_ref, latents.at[:, z], {"head": above})

    locals_[0].wait()
    locals_[1].wait()
    for slot in (HALO, HALO + 1, HALO + 2):
        arrived(slot)

    @pl.when(z == 0)
    def _():
        taps[:, 0] = jnp.zeros_like(taps[:, 0])

    total = jnp.zeros((128, 320), F32) + bias_ref[...]
    for ta in range(3):
        part = jnp.zeros((128, 320), F32)
        for tb in range(3):
            rows = jnp.concatenate(
                [taps[ta + d, 2 * r + tb] for d in range(2) for r in range(2)], axis=0
            )
            for te in range(3):
                part += lax.dot_general(
                    rows[:, te * 256 : (te + 1) * 256], conv_w[(ta * 3 + tb) * 3 + te],
                    (((1,), (1,)), ((), ())), preferred_element_type=F32,
                )
        keep = [
            (2 * f + d - 2 + ta >= clip_bounds(table, 2 * f + d)[0]).astype(F32) for d in range(2)
        ]
        row = lax.broadcasted_iota(jnp.int32, (128, 1), 0)
        total += part * jnp.where(row < 64, keep[0], keep[1])
    feature = total / (1.0 + jnp.exp(-total))
    feature = feature.reshape(4, 32, 320)[:, :24].reshape(2, 48, 320)
    feats[:, z] = feature.astype(BF16)
    for i, other in enumerate((below, above, across)):
        start(FEATURE + i, feats.at[:, z], feats.at[:, z], {"head": other})

    stage1(0)
    arrived(LATENT)
    start(LATENT + 2, latents.at[0, above], latents.at[0, above], {"head": below})
    arrived(LATENT + 1)
    start(LATENT + 3, latents.at[1, below], latents.at[1, below], {"head": above})

    def share(group, part):
        return wo_ref.at[pl.ds(5 * group, 5), :, pl.ds(1280 * part, 1280)]

    def send_share(slot, part, device):
        cols = pl.ds(pl.multiple_of(2560 * c + 1280 * part, 1280), 1280)
        start(slot, w_out_ref.at[:, :, cols], share(z, part), {"head": device})

    send_share(OUT, 0, below)
    send_share(OUT + 1, 1, above)
    stage2(0)
    for i in range(3):
        arrived(FEATURE + i)
    arrived(LATENT + 2)
    arrived(LATENT + 3)

    locals_[2].wait()
    locals_[3].wait()
    locals_[4].wait()

    feature_rows = feats[...].reshape(384, 320)
    for j in range(4):
        cols = pl.ds(1280 * j, 1280)
        value = latents[:, :, :, cols].reshape(384, 1280).astype(F32) + jnp.dot(
            feature_rows, proj[:, cols], preferred_element_type=F32
        )
        guided[j] = value.astype(BF16)

    t = pl.multiple_of(16 * lax.rem(f, THIRDS), 16)
    h = lax.div(f, THIRDS)

    def pushes(g, k):
        m = THIRDS * g + k
        common = dict(device_id={"frame": m}, device_id_type=MESH)
        return (
            pltpu.make_async_remote_copy(
                src_ref=qkv.at[pl.ds(3 * g + 1, 2)], dst_ref=kv_ref.at[f],
                send_sem=push_send.at[0, m], recv_sem=push_recv.at[0, f], **common,
            ),
            pltpu.make_async_remote_copy(
                src_ref=qkv.at[3 * g, :, :, pl.ds(16 * k, 16), :], dst_ref=q_ref.at[f],
                send_sem=push_send.at[1, m], recv_sem=push_recv.at[1, f], **common,
            ),
        )

    def stays(g, k):
        return (
            pltpu.make_async_copy(qkv.at[pl.ds(3 * g + 1, 2)], kv_ref.at[f], local.at[5]),
            pltpu.make_async_copy(qkv.at[3 * g, :, :, pl.ds(16 * k, 16), :], q_ref.at[f], local.at[6]),
        )

    stage3(0)
    for ia, ib in SIBLING_KEYS:
        slot = sibling_slot(0, ia, ib)
        there = region(0, place(1 - c, b + OFFSETS[ia], a + OFFSETS[ib]), 1 - c, 0)
        pltpu.make_async_remote_copy(
            src_ref=there, dst_ref=there, send_sem=send.at[slot], recv_sem=recv.at[slot],
            device_id={"dp": 1 - c}, device_id_type=MESH,
        ).wait_recv()

    def project(n, unused):
        g = lax.rem(f + n, HEADS_DEV)
        out = None
        for j in range(4):
            rows = pl.ds(1280 * j, 1280)
            rhs = jnp.concatenate([weights[3 * g + i, rows, :] for i in range(3)], axis=1)
            term = jnp.dot(guided[j], rhs, preferred_element_type=F32)
            out = term if out is None else out + term
        for i in range(3):
            qkv[3 * g + i] = out[:, 128 * i : 128 * (i + 1)].astype(BF16).reshape(2, 4, 48, 128)
        for k in range(THIRDS):
            m = THIRDS * g + k

            @pl.when(f != m)
            def _():
                for copy in pushes(g, k):
                    copy.start()

            @pl.when(f == m)
            def _():
                for copy in stays(g, k):
                    copy.start()

        return unused

    lax.fori_loop(0, 3, project, 0)
    arrived(OUT)
    start(OUT + 4, share(above, 0), share(above, 0), {"head": below})
    send_share(OUT + 2, 1, below)
    arrived(OUT + 1)
    start(OUT + 5, share(below, 1), share(below, 1), {"head": above})
    send_share(OUT + 3, 0, above)
    lax.fori_loop(3, HEADS_DEV, project, 0)

    attends = 1 - lax.div(f, n_frame - 1)

    def land(source, unused):
        @pl.when(source != f)
        def _():
            for ref, which in ((kv_ref, 0), (q_ref, 1)):
                pltpu.make_async_remote_copy(
                    src_ref=ref.at[source], dst_ref=ref.at[source],
                    send_sem=push_send.at[which, source], recv_sem=push_recv.at[which, source],
                    device_id={"frame": source}, device_id_type=MESH,
                ).wait_recv()

        @pl.when(source == f)
        def _():
            for copy in stays(0, 0):
                copy.wait()

        return unused

    lax.fori_loop(0, 2 * attends, land, 0)

    def turn(i, unused):
        values[i] = kv_ref[pl.ds(2 * i, 2), 1].reshape(768, 128).T
        return unused

    lax.fori_loop(0, attends, turn, 0)
    exponent = 1.4426950408889634 * 128 ** -0.5
    lane = lax.broadcasted_iota(jnp.int32, (1, 256), 1)

    def back(other):
        df, dz = lax.div(other, RING), lax.rem(other, RING)
        return pltpu.make_async_remote_copy(
            src_ref=mixed.at[df, :, dz], dst_ref=gathered.at[5 * z + h, :, pl.ds(t, 16), :],
            send_sem=back_send.at[other], recv_sem=back_recv.at[me],
            device_id={"frame": df, "head": dz}, device_id_type=MESH,
        )

    keep_own = pltpu.make_async_copy(
        mixed.at[f, :, z], gathered.at[5 * z + h, :, pl.ds(t, 16), :], local.at[8]
    )

    def tile(i, unused):
        more = 1 - lax.div(i, 7)
        lax.fori_loop(2 * i + 2, 2 * i + 2 + 2 * more, land, 0)
        lax.fori_loop(i + 1, i + 1 + more, turn, 0)
        queries = q_ref[pl.ds(2 * i, 2)].reshape(256, 128)
        low = jnp.zeros((1, 256), jnp.int32)
        high = jnp.zeros((1, 256), jnp.int32)
        for d in range(4):
            frame = 4 * i + d
            begin, end = clip_bounds(table, frame)
            block = table[8 + frame]
            later = (table[9 + frame] == block).astype(jnp.int32)
            later += (table[10 + frame] == block).astype(jnp.int32)
            inside = (lane >= 64 * d) & (lane < 64 * d + 64)
            low = jnp.where(inside, begin * 192, low)
            high = jnp.where(inside, jnp.minimum(end, frame + 1 + later) * 192, high)

        def chunk(j, carry):
            top, total, summed = carry
            keys = kv_ref[pl.ds(2 * j, 2), 0].reshape(768, 128)
            scores = lax.dot_general(
                keys, queries, (((1,), (1,)), ((), ())), preferred_element_type=F32
            )
            token = j * 768 + lax.broadcasted_iota(jnp.int32, (768, 256), 0)
            scores = jnp.where((token >= low) & (token < high), scores, MASKED)
            new = jnp.maximum(top, jnp.max(scores, axis=0, keepdims=True))
            factor = jnp.exp2((top - new) * exponent)
            weight = jnp.exp2((scores - new) * exponent)
            total = total * factor + jnp.sum(weight, axis=0, keepdims=True)
            summed = summed * factor + jnp.dot(
                values[j], weight.astype(BF16), preferred_element_type=F32
            )
            return new, total, summed

        carry = (
            jnp.full((1, 256), NEG_FILL, F32), jnp.zeros((1, 256), F32), jnp.zeros((128, 256), F32)
        )
        last = i + 2 - lax.div(i, 7)
        _, total, summed = lax.fori_loop(0, last, chunk, carry)
        rows = (summed / total).T.astype(BF16)
        mixed[pl.ds(2 * i, 2)] = rows.reshape(2, 2, 4, 16, 128)

        def give(e, unused):
            other = 8 * i + e

            @pl.when((f < n_frame - 1) & (other != me))
            def _():
                back(other).start()

            @pl.when((f < n_frame - 1) & (other == me))
            def _():
                keep_own.start()

            return unused

        lax.fori_loop(0, 8, give, 0)
        return unused

    lax.fori_loop(0, 8 * attends, tile, 0)
    for slot in range(OUT + 2, OUT + 6):
        arrived(slot)

    def half_cols(core, n):
        return pl.ds(pl.multiple_of(2560 * core + OUT_COLS * n, OUT_COLS), OUT_COLS)

    def fetch(n):
        cols = pl.ds(OUT_COLS * n, OUT_COLS)
        return [
            pltpu.make_async_copy(
                w_out_ref.at[:, :, half_cols(c, n)] if group is z
                else wo_ref.at[pl.ds(5 * group, 5), :, cols],
                wo_tiles.at[n % 2, pl.ds(5 * group, 5)],
                tile_sem.at[n % 2, i],
            )
            for i, group in enumerate((z, above, below, across))
        ]

    for copy in fetch(0) + fetch(1):
        copy.start()

    def collect(other, unused):
        @pl.when((f < n_frame - 1) & (other != me))
        def _():
            back(other).wait_send()

        @pl.when((f < n_frame - 1) & (other == me))
        def _():
            keep_own.wait()

        @pl.when((other < n_plane - RING) & (other != me))
        def _():
            df, dz = lax.div(other, RING), lax.rem(other, RING)
            place_of = gathered.at[5 * dz + lax.div(df, THIRDS), :, pl.ds(pl.multiple_of(16 * lax.rem(df, THIRDS), 16), 16), :]
            pltpu.make_async_remote_copy(
                src_ref=place_of, dst_ref=place_of,
                send_sem=back_send.at[other], recv_sem=back_recv.at[other],
                device_id={"frame": df, "head": dz}, device_id_type=MESH,
            ).wait_recv()

        return unused

    lax.fori_loop(0, n_plane, collect, 0)
    start(OUT + 6, gathered, gathered_other, {"dp": 1 - c})
    arrived(OUT + 6)
    lhs = jnp.concatenate(
        [
            jnp.concatenate([ref[n].reshape(96, 128) for n in range(20)], axis=1)
            for ref in (gathered, gathered_other)
        ],
        axis=0,
    )
    n_tiles = 2560 // OUT_COLS
    for n in range(n_tiles):
        for copy in fetch(n):
            copy.wait()
        out = jnp.dot(lhs, wo_tiles[n % 2].reshape(2560, OUT_COLS), preferred_element_type=F32)
        out = out.astype(BF16).reshape(4, 48, OUT_COLS)
        staged[n] = out[2:]
        start(OUT + 7 + n, staged.at[n], out_ref.at[:, :, half_cols(c, n)], {"dp": 1 - c})
        out_ref[:, :, half_cols(c, n)] = out[:2]
        if n + 2 < n_tiles:
            for copy in fetch(n + 2):
                copy.start()
    for n in range(n_tiles):
        arrived(OUT + 7 + n)
    for copy in copies.values():
        copy.wait_send()
    for g in range(HEADS_DEV):
        for k in range(THIRDS):

            @pl.when(f != THIRDS * g + k)
            def _():
                for copy in pushes(g, k):
                    copy.wait_send()


def shards(
    latent, pose_maps, conv_weight, conv_bias, pose_proj, w_qkv, w_out, clip_lengths, block_ids
):
    frames_dev, rows_in, cols_in, c_in = pose_maps.shape
    cols = cols_in // 2
    pairs = pose_maps.reshape(frames_dev, rows_in, cols, 2 * c_in)
    left = jnp.pad(pairs[:, :, :-1, c_in:], ((0, 0), (0, 0), (1, 0), (0, 0)))
    own = jnp.concatenate([left, pairs], axis=3)
    own = jnp.pad(own, ((0, 0), (0, 0), (0, 32 - cols), (0, 0)))
    c_out = conv_weight.shape[-1]
    kernel = jnp.transpose(conv_weight, (0, 1, 2, 4, 3)).reshape(27, c_out, c_in)
    weight = jnp.transpose(w_qkv, (1, 2, 0, 3)).reshape(15, 320, 128)
    table = jnp.concatenate(
        [clip_lengths, jnp.zeros((5,), jnp.int32), block_ids, jnp.full((8,), -1, jnp.int32)]
    )
    hbm = pl.BlockSpec(memory_space=pl.ANY)
    vmem = pl.BlockSpec(memory_space=pltpu.VMEM)
    attended, _ = pl.pallas_call(
        gather_kernel,
        out_shape=(
            jax.ShapeDtypeStruct((2, 48, 5120), BF16),
            jax.ShapeDtypeStruct((20, 128, 2560), BF16),
        ),
        in_specs=[pl.BlockSpec(memory_space=pltpu.SMEM)] + [hbm] * 6 + [vmem],
        out_specs=(vmem, hbm),
        scratch_shapes=[
            pltpu.VMEM((4, 5, 32, 768), BF16),
            pltpu.VMEM((2, 4, 48, 5120), BF16),
            pltpu.VMEM((15, 5120, 128), BF16),
            pltpu.VMEM((27, c_out, c_in), BF16),
            pltpu.VMEM((320, 5120), BF16),
            pltpu.VMEM((2, 4, 48, 320), BF16),
            pltpu.VMEM((4, 384, 1280), BF16),
            pltpu.VMEM((15, 2, 4, 48, 128), BF16),
            pltpu.VMEM((16, 2, 2, 4, 48, 128), BF16),
            pltpu.VMEM((16, 2, 4, 16, 128), BF16),
            pltpu.VMEM((8, 128, 768), BF16),
            pltpu.VMEM((16, 2, 4, 16, 128), BF16),
            pltpu.VMEM((20, 2, 48, 128), BF16),
            pltpu.VMEM((20, 2, 48, 128), BF16),
            pltpu.VMEM((2, 20, 128, OUT_COLS), BF16),
            pltpu.VMEM((2560 // OUT_COLS, 2, 48, OUT_COLS), BF16),
            pltpu.SemaphoreType.DMA((COPIES,)),
            pltpu.SemaphoreType.DMA((COPIES,)),
            pltpu.SemaphoreType.DMA((9,)),
            pltpu.SemaphoreType.DMA((2, 16)),
            pltpu.SemaphoreType.DMA((2, 16)),
            pltpu.SemaphoreType.DMA((64,)),
            pltpu.SemaphoreType.DMA((64,)),
            pltpu.SemaphoreType.DMA((2, 4)),
        ],
        compiler_params=pltpu.CompilerParams(
            collective_id=0, has_side_effects=True, vmem_limit_bytes=60 << 20
        ),
        name="gather_project_attend",
    )(
        table, own, latent.reshape(2, 48, 5120), weight, kernel, pose_proj, w_out,
        conv_bias[None, :],
    )
    return attended.reshape(latent.shape)


def solution(mesh):
    return jax.shard_map(
        shards,
        mesh=mesh,
        in_specs=(
            P(("dp", "frame"), "head", None, None),
            P(("dp", "frame"), "head", None, None),
            P(),
            P(),
            P(),
            P("frame", "head", None, None),
            P("head", None, None),
            P("dp"),
            P("dp"),
        ),
        out_specs=P(("dp", "frame"), "head", None, None),
        check_vma=False,
    )
```

```python
import jax
import jax.numpy as jnp
from jax import lax
from jax.experimental import pallas as pl
from jax.experimental.pallas import tpu as pltpu
from jax.sharding import PartitionSpec as P

NEG_FILL = -1e30
F32 = jnp.float32
BF16 = jnp.bfloat16
THIRDS = 3
MESH = pl.DeviceIdType.MESH
RING = 4
OFFSETS = (0, RING - 1, 1, 2)
PARTS = ((0, 160), (0, 80), (80, 80))
HALO, LATENT, FEATURE, OUT, WEIGHT = 0, 3, 7, 10, 22
RING_KEYS = [(i, 0, 0) for i in (1, 2, 3)] + [
    (i, j, part) for i in range(4) for j, part in ((1, 0), (2, 0), (3, 1), (3, 2))
]
SIBLING_KEYS = [(i, j) for i in range(4) for j in range(4) if i or j]
CHUNK = len(RING_KEYS) + len(SIBLING_KEYS)
CHUNKS = 1
HEADS_DEV = 5
COPIES = WEIGHT + CHUNKS * CHUNK
MASKED = -3e30
OUT_COLS = 512


def clip_bounds(table, frame):
    first = table[0]
    second = first + table[1]
    start = jnp.where(frame >= second, second, jnp.where(frame >= first, first, 0))
    stop = jnp.where(frame >= second, second + table[2], jnp.where(frame >= first, second, first))
    return start, stop


def gather_kernel(
    table, blocks, own_ref, latent_ref, weight_ref, conv_ref, proj_ref, w_out_ref, bias_ref,
    out_ref, wo_ref,
    taps, latents, weights, conv_w, proj, feats, guided, qkv,
    kv_ref, q_ref, values, mixed, gathered, gathered_other, wo_tiles, staged,
    send, recv, local, push_send, push_recv, back_send, back_recv, tile_sem,
):
    f, z, c = lax.axis_index("frame"), lax.axis_index("head"), lax.axis_index("dp")
    x, y = lax.rem(f, RING), lax.div(f, RING)
    a, b = x + c * (y - x), y + c * (x - y)
    n_frame = RING * RING
    ahead, behind = lax.rem(f + 1, n_frame), lax.rem(f + n_frame - 1, n_frame)
    below, above, across = lax.rem(z + 1, RING), lax.rem(z + RING - 1, RING), lax.rem(z + 2, RING)

    def place(core, va, vb):
        va, vb = lax.rem(va, RING), lax.rem(vb, RING)
        return (vb + core * (va - vb)) * RING + va + core * (vb - va)

    locals_ = [
        pltpu.make_async_copy(own_ref, taps.at[pl.ds(2, 2), pl.ds(1, 4)], local.at[0]),
        pltpu.make_async_copy(conv_ref, conv_w, local.at[1]),
        pltpu.make_async_copy(proj_ref, proj, local.at[2]),
        pltpu.make_async_copy(latent_ref, latents.at[:, z], local.at[3]),
        pltpu.make_async_copy(
            weight_ref, weights.at[:, pl.ds(pl.multiple_of(f * 320, 320), 320), :], local.at[4]
        ),
    ]
    for copy in locals_:
        copy.start()

    barrier = pltpu.get_barrier_semaphore()

    me = RING * f + z
    n_plane = RING * n_frame

    def greet(j, unused):
        other = lax.rem(me + j, n_plane)
        pl.semaphore_signal(
            barrier, inc=1,
            device_id={"frame": lax.div(other, RING), "head": lax.rem(other, RING)},
            device_id_type=MESH,
        )
        return unused

    lax.fori_loop(1, n_plane, greet, 0)
    pl.semaphore_signal(barrier, inc=1, device_id={"dp": 1 - c}, device_id_type=MESH)
    pl.semaphore_wait(barrier, n_plane)

    copies = {}

    def start(slot, src, dst, device):
        copy = pltpu.make_async_remote_copy(
            src_ref=src, dst_ref=dst, send_sem=send.at[slot], recv_sem=recv.at[slot],
            device_id=device, device_id_type=MESH,
        )
        copy.start()
        copies[slot] = copy

    def arrived(slot):
        copies[slot].wait_recv()

    start(HALO, own_ref, taps.at[pl.ds(0, 2), pl.ds(1, 4)], {"frame": ahead})
    start(HALO + 1, own_ref.at[:, pl.ds(3, 1)], taps.at[pl.ds(2, 2), pl.ds(0, 1)], {"head": below})
    start(
        HALO + 2, own_ref.at[:, pl.ds(3, 1)], taps.at[pl.ds(0, 2), pl.ds(0, 1)],
        {"frame": ahead, "head": below},
    )

    def region(g, shard, core, part):
        offset, rows = PARTS[part]
        first = pl.multiple_of(shard * 320 + core * 160 + offset, 16)
        return weights.at[:, pl.ds(first, rows), :]

    def slot_of(g, ia, ib, part):
        return WEIGHT + CHUNK * g + RING_KEYS.index((ia, ib, part))

    def sibling_slot(g, ia, ib):
        return WEIGHT + CHUNK * g + len(RING_KEYS) + SIBLING_KEYS.index((ia, ib))

    def pass_on(g, ia, ib, axis, step, part):
        shard = place(c, a + OFFSETS[ia], b + OFFSETS[ib])
        go = step % RING
        device = place(c, a + go, b) if axis == 0 else place(c, a, b + go)
        was = ia if axis == 0 else ib
        now = {1: 1, -1: 2, 2: 3}[step] if was == 0 else 3
        there = (now, ib) if axis == 0 else (ia, now)
        src = region(g, shard, c, part)
        if ia == 0 and ib == 0:
            src = weight_ref.at[:, pl.ds(pl.multiple_of(c * 160, 160), 160), :]
        start(slot_of(g, *there, part), src, region(g, shard, c, part), {"frame": device})

    def to_sibling(g, ia, ib):
        shard = place(c, a + OFFSETS[ia], b + OFFSETS[ib])
        here = region(g, shard, c, 0)
        start(sibling_slot(g, ia, ib), here, here, {"dp": 1 - c})

    def second_ring(g, ia):
        for ib, step, part in ((1, 1, 1), (2, -1, 2)):
            arrived(slot_of(g, ia, ib, 0))
            pass_on(g, ia, ib, 1, step, part)
            to_sibling(g, ia, ib)

    def last_shard(g, ia):
        arrived(slot_of(g, ia, 3, 1))
        arrived(slot_of(g, ia, 3, 2))
        to_sibling(g, ia, 3)

    def stage0(g):
        for step in (1, -1, 2):
            pass_on(g, 0, 0, 0, step, 0)
        for step in (1, -1):
            pass_on(g, 0, 0, 1, step, 0)

    def stage1(g):
        for ia in (1, 2, 3):
            arrived(slot_of(g, ia, 0, 0))
            pass_on(g, ia, 0, 1, 1, 0)
            pass_on(g, ia, 0, 1, -1, 0)
            to_sibling(g, ia, 0)
        second_ring(g, 0)

    def stage2(g):
        for ia in (1, 2, 3):
            second_ring(g, ia)
        last_shard(g, 0)

    def stage3(g):
        for ia in (1, 2, 3):
            last_shard(g, ia)

    stage0(0)
    start(LATENT, latent_ref, latents.at[:, z], {"head": below})
    start(LATENT + 1, latent_ref, latents.at[:, z], {"head": above})

    locals_[0].wait()
    locals_[1].wait()
    for slot in (HALO, HALO + 1, HALO + 2):
        arrived(slot)

    @pl.when(z == 0)
    def _():
        taps[:, 0] = jnp.zeros_like(taps[:, 0])

    total = jnp.zeros((128, 320), F32) + bias_ref[...]
    for ta in range(3):
        part = jnp.zeros((128, 320), F32)
        for tb in range(3):
            rows = jnp.concatenate(
                [taps[ta + d, 2 * r + tb] for d in range(2) for r in range(2)], axis=0
            )
            for te in range(3):
                part += lax.dot_general(
                    rows[:, te * 256 : (te + 1) * 256], conv_w[(ta * 3 + tb) * 3 + te],
                    (((1,), (1,)), ((), ())), preferred_element_type=F32,
                )
        keep = [
            (2 * f + d - 2 + ta >= clip_bounds(table, 2 * f + d)[0]).astype(F32) for d in range(2)
        ]
        row = lax.broadcasted_iota(jnp.int32, (128, 1), 0)
        total += part * jnp.where(row < 64, keep[0], keep[1])
    feature = total / (1.0 + jnp.exp(-total))
    feature = feature.reshape(4, 32, 320)[:, :24].reshape(2, 48, 320)
    feats[:, z] = feature.astype(BF16)
    for i, other in enumerate((below, above, across)):
        start(FEATURE + i, feats.at[:, z], feats.at[:, z], {"head": other})

    stage1(0)
    arrived(LATENT)
    start(LATENT + 2, latents.at[0, above], latents.at[0, above], {"head": below})
    arrived(LATENT + 1)
    start(LATENT + 3, latents.at[1, below], latents.at[1, below], {"head": above})

    def share(group, part):
        return wo_ref.at[pl.ds(5 * group, 5), :, pl.ds(1280 * part, 1280)]

    def send_share(slot, part, device):
        cols = pl.ds(pl.multiple_of(2560 * c + 1280 * part, 1280), 1280)
        start(slot, w_out_ref.at[:, :, cols], share(z, part), {"head": device})

    send_share(OUT, 0, below)
    send_share(OUT + 1, 1, above)
    stage2(0)
    for i in range(3):
        arrived(FEATURE + i)
    arrived(LATENT + 2)
    arrived(LATENT + 3)

    locals_[2].wait()
    locals_[3].wait()
    locals_[4].wait()

    feature_rows = feats[...].reshape(384, 320)
    for j in range(4):
        cols = pl.ds(1280 * j, 1280)
        value = latents[:, :, :, cols].reshape(384, 1280).astype(F32) + jnp.dot(
            feature_rows, proj[:, cols], preferred_element_type=F32
        )
        guided[j] = value.astype(BF16)

    t = pl.multiple_of(16 * lax.rem(f, THIRDS), 16)
    h = lax.div(f, THIRDS)

    def pushes(g, k):
        m = THIRDS * g + k
        common = dict(device_id={"frame": m}, device_id_type=MESH)
        return (
            pltpu.make_async_remote_copy(
                src_ref=qkv.at[pl.ds(3 * g + 1, 2)], dst_ref=kv_ref.at[f],
                send_sem=push_send.at[0, m], recv_sem=push_recv.at[0, f], **common,
            ),
            pltpu.make_async_remote_copy(
                src_ref=qkv.at[3 * g, :, :, pl.ds(16 * k, 16), :], dst_ref=q_ref.at[f],
                send_sem=push_send.at[1, m], recv_sem=push_recv.at[1, f], **common,
            ),
        )

    def stays(g, k):
        return (
            pltpu.make_async_copy(qkv.at[pl.ds(3 * g + 1, 2)], kv_ref.at[f], local.at[5]),
            pltpu.make_async_copy(qkv.at[3 * g, :, :, pl.ds(16 * k, 16), :], q_ref.at[f], local.at[6]),
        )

    stage3(0)
    for ia, ib in SIBLING_KEYS:
        slot = sibling_slot(0, ia, ib)
        there = region(0, place(1 - c, b + OFFSETS[ia], a + OFFSETS[ib]), 1 - c, 0)
        pltpu.make_async_remote_copy(
            src_ref=there, dst_ref=there, send_sem=send.at[slot], recv_sem=recv.at[slot],
            device_id={"dp": 1 - c}, device_id_type=MESH,
        ).wait_recv()

    def project(n, unused):
        g = lax.rem(f + n, HEADS_DEV)
        out = None
        for j in range(4):
            rows = pl.ds(1280 * j, 1280)
            rhs = jnp.concatenate([weights[3 * g + i, rows, :] for i in range(3)], axis=1)
            term = jnp.dot(guided[j], rhs, preferred_element_type=F32)
            out = term if out is None else out + term
        for i in range(3):
            qkv[3 * g + i] = out[:, 128 * i : 128 * (i + 1)].astype(BF16).reshape(2, 4, 48, 128)
        for k in range(THIRDS):
            m = THIRDS * g + k

            @pl.when(f != m)
            def _():
                for copy in pushes(g, k):
                    copy.start()

            @pl.when(f == m)
            def _():
                for copy in stays(g, k):
                    copy.start()

        return unused

    lax.fori_loop(0, 3, project, 0)
    arrived(OUT)
    start(OUT + 4, share(above, 0), share(above, 0), {"head": below})
    send_share(OUT + 2, 1, below)
    arrived(OUT + 1)
    start(OUT + 5, share(below, 1), share(below, 1), {"head": above})
    send_share(OUT + 3, 0, above)
    lax.fori_loop(3, HEADS_DEV, project, 0)

    attends = 1 - lax.div(f, n_frame - 1)

    def land(source, unused):
        @pl.when(source != f)
        def _():
            for ref, which in ((kv_ref, 0), (q_ref, 1)):
                pltpu.make_async_remote_copy(
                    src_ref=ref.at[source], dst_ref=ref.at[source],
                    send_sem=push_send.at[which, source], recv_sem=push_recv.at[which, source],
                    device_id={"frame": source}, device_id_type=MESH,
                ).wait_recv()

        @pl.when(source == f)
        def _():
            for copy in stays(0, 0):
                copy.wait()

        return unused

    lax.fori_loop(0, 2 * attends, land, 0)

    def turn(i, unused):
        values[i] = kv_ref[pl.ds(2 * i, 2), 1].reshape(768, 128).T
        return unused

    lax.fori_loop(0, attends, turn, 0)
    exponent = 1.4426950408889634 * 128 ** -0.5
    lane = lax.broadcasted_iota(jnp.int32, (1, 256), 1)

    def back(other):
        df, dz = lax.div(other, RING), lax.rem(other, RING)
        return pltpu.make_async_remote_copy(
            src_ref=mixed.at[df, :, dz], dst_ref=gathered.at[5 * z + h, :, pl.ds(t, 16), :],
            send_sem=back_send.at[other], recv_sem=back_recv.at[me],
            device_id={"frame": df, "head": dz}, device_id_type=MESH,
        )

    keep_own = pltpu.make_async_copy(
        mixed.at[f, :, z], gathered.at[5 * z + h, :, pl.ds(t, 16), :], local.at[8]
    )

    def tile(i, unused):
        more = 1 - lax.div(i, 7)
        lax.fori_loop(2 * i + 2, 2 * i + 2 + 2 * more, land, 0)
        lax.fori_loop(i + 1, i + 1 + more, turn, 0)
        queries = q_ref[pl.ds(2 * i, 2)].reshape(256, 128)
        low = jnp.zeros((1, 256), jnp.int32)
        high = jnp.zeros((1, 256), jnp.int32)
        for d in range(4):
            frame = 4 * i + d
            begin, end = clip_bounds(table, frame)
            block = blocks[frame]
            one = frame + 1 - lax.div(frame + 1, 32)
            two = frame + 2 - lax.div(frame + 2, 32) * (frame - 29)
            later = (blocks[one] == block).astype(jnp.int32)
            later += (blocks[two] == block).astype(jnp.int32)
            inside = (lane >= 64 * d) & (lane < 64 * d + 64)
            low = jnp.where(inside, begin * 192, low)
            high = jnp.where(inside, jnp.minimum(end, frame + 1 + later) * 192, high)

        def chunk(j, carry):
            top, total, summed = carry
            keys = kv_ref[pl.ds(2 * j, 2), 0].reshape(768, 128)
            scores = lax.dot_general(
                keys, queries, (((1,), (1,)), ((), ())), preferred_element_type=F32
            )
            token = j * 768 + lax.broadcasted_iota(jnp.int32, (768, 256), 0)
            scores = jnp.where((token >= low) & (token < high), scores, MASKED)
            new = jnp.maximum(top, jnp.max(scores, axis=0, keepdims=True))
            factor = jnp.exp2((top - new) * exponent)
            weight = jnp.exp2((scores - new) * exponent)
            total = total * factor + jnp.sum(weight, axis=0, keepdims=True)
            summed = summed * factor + jnp.dot(
                values[j], weight.astype(BF16), preferred_element_type=F32
            )
            return new, total, summed

        carry = (
            jnp.full((1, 256), NEG_FILL, F32), jnp.zeros((1, 256), F32), jnp.zeros((128, 256), F32)
        )
        last = i + 2 - lax.div(i, 7)
        _, total, summed = lax.fori_loop(0, last, chunk, carry)
        rows = (summed / total).T.astype(BF16)
        mixed[pl.ds(2 * i, 2)] = rows.reshape(2, 2, 4, 16, 128)

        def give(e, unused):
            other = 8 * i + e

            @pl.when((f < n_frame - 1) & (other != me))
            def _():
                back(other).start()

            @pl.when((f < n_frame - 1) & (other == me))
            def _():
                keep_own.start()

            return unused

        lax.fori_loop(0, 8, give, 0)
        return unused

    lax.fori_loop(0, 8 * attends, tile, 0)
    for slot in range(OUT + 2, OUT + 6):
        arrived(slot)

    def half_cols(core, n):
        return pl.ds(pl.multiple_of(2560 * core + OUT_COLS * n, OUT_COLS), OUT_COLS)

    def fetch(n):
        cols = pl.ds(OUT_COLS * n, OUT_COLS)
        return [
            pltpu.make_async_copy(
                w_out_ref.at[:, :, half_cols(c, n)] if group is z
                else wo_ref.at[pl.ds(5 * group, 5), :, cols],
                wo_tiles.at[n % 2, pl.ds(5 * group, 5)],
                tile_sem.at[n % 2, i],
            )
            for i, group in enumerate((z, above, below, across))
        ]

    for copy in fetch(0) + fetch(1):
        copy.start()

    def collect(other, unused):
        @pl.when((f < n_frame - 1) & (other != me))
        def _():
            back(other).wait_send()

        @pl.when((f < n_frame - 1) & (other == me))
        def _():
            keep_own.wait()

        @pl.when((other < n_plane - RING) & (other != me))
        def _():
            df, dz = lax.div(other, RING), lax.rem(other, RING)
            place_of = gathered.at[5 * dz + lax.div(df, THIRDS), :, pl.ds(pl.multiple_of(16 * lax.rem(df, THIRDS), 16), 16), :]
            pltpu.make_async_remote_copy(
                src_ref=place_of, dst_ref=place_of,
                send_sem=back_send.at[other], recv_sem=back_recv.at[other],
                device_id={"frame": df, "head": dz}, device_id_type=MESH,
            ).wait_recv()

        return unused

    lax.fori_loop(0, n_plane, collect, 0)
    start(OUT + 6, gathered, gathered_other, {"dp": 1 - c})
    arrived(OUT + 6)
    lhs = jnp.concatenate(
        [
            jnp.concatenate([ref[n].reshape(96, 128) for n in range(20)], axis=1)
            for ref in (gathered, gathered_other)
        ],
        axis=0,
    )
    n_tiles = 2560 // OUT_COLS
    for n in range(n_tiles):
        for copy in fetch(n):
            copy.wait()
        out = jnp.dot(lhs, wo_tiles[n % 2].reshape(2560, OUT_COLS), preferred_element_type=F32)
        out = out.astype(BF16).reshape(4, 48, OUT_COLS)
        staged[n] = out[2:]
        start(OUT + 7 + n, staged.at[n], out_ref.at[:, :, half_cols(c, n)], {"dp": 1 - c})
        out_ref[:, :, half_cols(c, n)] = out[:2]
        if n + 2 < n_tiles:
            for copy in fetch(n + 2):
                copy.start()
    for n in range(n_tiles):
        arrived(OUT + 7 + n)
    for copy in copies.values():
        copy.wait_send()
    for g in range(HEADS_DEV):
        for k in range(THIRDS):

            @pl.when(f != THIRDS * g + k)
            def _():
                for copy in pushes(g, k):
                    copy.wait_send()


def shards(
    latent, pose_maps, conv_weight, conv_bias, pose_proj, w_qkv, w_out, clip_lengths, block_ids
):
    frames_dev, rows_in, cols_in, c_in = pose_maps.shape
    cols = cols_in // 2
    pairs = pose_maps.reshape(frames_dev, rows_in, cols, 2 * c_in)
    left = jnp.pad(pairs[:, :, :-1, c_in:], ((0, 0), (0, 0), (1, 0), (0, 0)))
    own = jnp.concatenate([left, pairs], axis=3)
    own = jnp.pad(own, ((0, 0), (0, 0), (0, 32 - cols), (0, 0)))
    c_out = conv_weight.shape[-1]
    kernel = jnp.transpose(conv_weight, (0, 1, 2, 4, 3)).reshape(27, c_out, c_in)
    weight = jnp.transpose(w_qkv, (1, 2, 0, 3)).reshape(15, 320, 128)
    hbm = pl.BlockSpec(memory_space=pl.ANY)
    vmem = pl.BlockSpec(memory_space=pltpu.VMEM)
    attended, _ = pl.pallas_call(
        gather_kernel,
        out_shape=(
            jax.ShapeDtypeStruct((2, 48, 5120), BF16),
            jax.ShapeDtypeStruct((20, 128, 2560), BF16),
        ),
        in_specs=[pl.BlockSpec(memory_space=pltpu.SMEM)] * 2 + [hbm] * 6 + [vmem],
        out_specs=(vmem, hbm),
        scratch_shapes=[
            pltpu.VMEM((4, 5, 32, 768), BF16),
            pltpu.VMEM((2, 4, 48, 5120), BF16),
            pltpu.VMEM((15, 5120, 128), BF16),
            pltpu.VMEM((27, c_out, c_in), BF16),
            pltpu.VMEM((320, 5120), BF16),
            pltpu.VMEM((2, 4, 48, 320), BF16),
            pltpu.VMEM((4, 384, 1280), BF16),
            pltpu.VMEM((15, 2, 4, 48, 128), BF16),
            pltpu.VMEM((16, 2, 2, 4, 48, 128), BF16),
            pltpu.VMEM((16, 2, 4, 16, 128), BF16),
            pltpu.VMEM((8, 128, 768), BF16),
            pltpu.VMEM((16, 2, 4, 16, 128), BF16),
            pltpu.VMEM((20, 2, 48, 128), BF16),
            pltpu.VMEM((20, 2, 48, 128), BF16),
            pltpu.VMEM((2, 20, 128, OUT_COLS), BF16),
            pltpu.VMEM((2560 // OUT_COLS, 2, 48, OUT_COLS), BF16),
            pltpu.SemaphoreType.DMA((COPIES,)),
            pltpu.SemaphoreType.DMA((COPIES,)),
            pltpu.SemaphoreType.DMA((9,)),
            pltpu.SemaphoreType.DMA((2, 16)),
            pltpu.SemaphoreType.DMA((2, 16)),
            pltpu.SemaphoreType.DMA((64,)),
            pltpu.SemaphoreType.DMA((64,)),
            pltpu.SemaphoreType.DMA((2, 4)),
        ],
        compiler_params=pltpu.CompilerParams(
            collective_id=0, has_side_effects=True, vmem_limit_bytes=60 << 20
        ),
        name="gather_project_attend",
    )(
        clip_lengths, block_ids, own, latent.reshape(2, 48, 5120), weight, kernel, pose_proj, w_out,
        conv_bias[None, :],
    )
    return attended.reshape(latent.shape)


def solution(mesh):
    return jax.shard_map(
        shards,
        mesh=mesh,
        in_specs=(
            P(("dp", "frame"), "head", None, None),
            P(("dp", "frame"), "head", None, None),
            P(),
            P(),
            P(),
            P("frame", "head", None, None),
            P("head", None, None),
            P("dp"),
            P("dp"),
        ),
        out_specs=P(("dp", "frame"), "head", None, None),
        check_vma=False,
    )
```
